32 devices in a mesh: stat: 16 (over z, x, core), tm: 2 (over y).
Axes of the slice: x: 2, y: 2, z: 4, core: 2. Of those that a mesh axis runs over, the one named last changes fastest.
Arguments:
- voltages: bfloat16 [2, 1024, 8, 4096], P(None, 'stat', 'tm'), may hold values from -6 to 6
- beam_weights: bfloat16 [2, 1024, 256], P(None, 'stat'), may hold values from -0.125 to 0.125
Outputs:
- beams: bfloat16 [4096, 8, 2, 256], P('stat', 'tm')
- visibilities: float32 [1024, 32, 2, 1024], P('tm', 'stat')
The draws below stay inside these ranges and needn't reach their ends.
All inputs are finite; a program needn't handle non-finite values.
Results may differ from the reference program's by a relative error of at most 0.011.
Values may be sent and summed in bfloat16 or wider, within the bound.
A program may use at most 64 MiB of HBM per device.

```python
import jax
import jax.numpy as jnp
from jax import lax

INPUTS = 1024
NA = 16
NB = 256
BEAMS = 256
AVG = 128
NF = 4096
SPEC = 8
VCH = 32
N_STAT = 16


def shard_levels(own_key, dims, cuts, low, largest):
    gain = 1.0
    for position, parts in cuts:
        draws = jax.random.uniform(jax.random.fold_in(jax.random.fold_in(own_key, 6), position), (parts,), jnp.float32, low / len(cuts), largest / len(cuts))
        gain = gain * jnp.repeat(jnp.exp(draws), dims[position] // parts).reshape((-1,) + (1,) * (len(dims) - 1 - position))
    return gain


def gaussian(stream_key, dims, scale, limit, shards=(), kind=jnp.bfloat16):
    level = shard_levels(stream_key, dims, shards, -0.22, 0.18) if shards else 1.0
    array = jax.random.normal(stream_key, dims, jnp.float32) * scale * level
    return jnp.minimum(jnp.maximum(array, -limit), limit).astype(kind)


def setup_inputs(seed: int = 0) -> dict:
    arg_keys = jax.random.split(jax.random.key(seed), 3)
    return {
        "voltages": gaussian(arg_keys[0], (2, INPUTS, SPEC, NF), 1.0, 6.0, ((1, 16), (2, 2))),
        "beam_weights": gaussian(arg_keys[1], (2, INPUTS, BEAMS), (2 * INPUTS) ** -0.5, 0.125, ((1, 16),)),
    }


def block_spectra(volt_block):
    signal = volt_block[0].astype(jnp.float32) + 1j * volt_block[1].astype(jnp.float32)
    transform = jnp.fft.fft(signal, axis=-1, norm="ortho")
    return jnp.stack([jnp.real(transform), jnp.imag(transform)]).astype(jnp.bfloat16)


def reference(voltages, beam_weights):
    block_width = INPUTS // N_STAT
    total_channels = NA * NB
    grouped = voltages.reshape(2, N_STAT, block_width, SPEC, total_channels).transpose(1, 0, 2, 3, 4)
    spectra = lax.map(block_spectra, grouped)
    weight_stack = jnp.stack([jnp.stack([beam_weights[0], beam_weights[1]], 1), jnp.stack([-beam_weights[1], beam_weights[0]], 1)], 0)
    weight_blocks = weight_stack.reshape(2, N_STAT, block_width, 2, BEAMS).transpose(1, 0, 2, 3, 4)

    def add_block(running, pair):
        spec_block, weight_block = pair
        partial_value = jnp.einsum('pisc,piqb->csqb', spec_block.astype(jnp.float32), weight_block.astype(jnp.float32))
        rounded = lax.optimization_barrier(partial_value.astype(jnp.bfloat16))
        return running + rounded.astype(jnp.float32), None

    beam_total, _ = lax.scan(add_block, jnp.zeros((total_channels, SPEC, 2, BEAMS), jnp.float32), (spectra, weight_blocks))
    beams = beam_total.astype(jnp.bfloat16)
    all_spectra = spectra.transpose(1, 0, 2, 3, 4).reshape(2, INPUTS, SPEC, total_channels)
    scale = 1.0 / (SPEC * AVG)

    def one_channel(channel_index):
        band = lax.dynamic_slice_in_dim(all_spectra, channel_index * AVG, AVG, 3).astype(jnp.float32)
        real_gram = jnp.einsum('pisc,pjsc->ij', band, band)
        mixed = jnp.einsum('isc,jsc->ij', band[1], band[0])
        return jnp.stack([real_gram, mixed - mixed.T]) * scale

    stacked = lax.map(one_channel, jnp.arange(VCH, dtype=jnp.int32))
    visibilities = stacked.transpose(2, 0, 1, 3)
    return beams, visibilities
```

```python
import functools
import math

import jax
import jax.numpy as jnp
import numpy as np
from jax import lax
from jax.experimental import pallas as pl
from jax.experimental.pallas import tpu as pltpu
from jax.sharding import PartitionSpec as P

NA = 16
NB = 256
AVG = 128


def dft_block(length):
    index = jnp.arange(length, dtype=jnp.int32)
    product = index[:, None] * index[None, :] % length
    angle = product.astype(jnp.float32) * (2.0 * math.pi / length)
    cosine = jnp.cos(angle)
    sine = jnp.sin(angle)
    return jnp.stack([jnp.stack([cosine, -sine]), jnp.stack([sine, cosine])])


def fine_spectra(voltages):
    block_inputs = voltages.shape[1]
    spectra_count = voltages.shape[2]
    signal = voltages.astype(jnp.float32).reshape(2, block_inputs, spectra_count, NA, NB)
    first = jnp.einsum("poak,pisab->osikb", dft_block(NA), signal, precision=lax.Precision.HIGH)
    outer_index = jnp.arange(NA, dtype=jnp.int32)
    inner_index = jnp.arange(NB, dtype=jnp.int32)
    rotation = (outer_index[:, None] * inner_index[None, :] % (NA * NB)).astype(jnp.float32) * (
        2.0 * math.pi / (NA * NB)
    )
    cos_twist = jnp.cos(rotation)
    sin_twist = jnp.sin(rotation)
    rotated = jnp.stack(
        [first[0] * cos_twist + first[1] * sin_twist, first[1] * cos_twist - first[0] * sin_twist]
    )
    final = jnp.einsum("osikb,ocbq->csiqk", rotated, dft_block(NB), precision=lax.Precision.HIGH)
    norm_factor = 1.0 / math.sqrt(NA * NB)
    return (
        (final * norm_factor).reshape(2, spectra_count, block_inputs, NA * NB).astype(jnp.bfloat16)
    )


def stack_weights(weights):
    return jnp.stack(
        [jnp.stack([weights[0], weights[1]], 1), jnp.stack([-weights[1], weights[0]], 1)], 0
    )


def body(voltages, beam_weights):
    stat_count = lax.axis_size("stat")
    time_count = lax.axis_size("tm")
    block_inputs = voltages.shape[1]
    spectra = fine_spectra(voltages)
    spectra_count = spectra.shape[1]
    channel_share = NA * NB // stat_count
    all_weights = lax.all_gather(beam_weights, "stat", axis=1, tiled=True)
    full_stack = stack_weights(all_weights)
    turned = lax.all_to_all(spectra, "stat", split_axis=3, concat_axis=2, tiled=True)
    item_count = turned.shape[1]

    def add_block(block_index, running):
        offset = (block_index * block_inputs).astype(jnp.int32)
        spec_block = lax.dynamic_slice_in_dim(turned, offset, block_inputs, 2)
        weight_block = lax.dynamic_slice_in_dim(full_stack, offset, block_inputs, 1)
        partial_value = jnp.einsum(
            "psic,piqb->csqb", spec_block, weight_block, preferred_element_type=jnp.float32
        )
        rounded = lax.optimization_barrier(partial_value.astype(jnp.bfloat16))
        return running + rounded.astype(jnp.float32)

    initial = jnp.zeros((turned.shape[3], item_count, 2, beam_weights.shape[2]), jnp.float32)
    beams = lax.fori_loop(0, stat_count, add_block, initial).astype(jnp.bfloat16)
    local_vch = channel_share // AVG
    scale = 1.0 / (spectra_count * time_count * AVG)
    split = turned.reshape(2, spectra_count, stat_count * block_inputs, local_vch, AVG)
    real_gram = jnp.einsum("psiva,psjva->ivj", split, split, preferred_element_type=jnp.float32)
    mixed = jnp.einsum("siva,sjva->ivj", split[1], split[0], preferred_element_type=jnp.float32)
    mixed = mixed - jnp.einsum(
        "siva,sjva->ivj", split[0], split[1], preferred_element_type=jnp.float32
    )
    visibilities = lax.psum_scatter(
        (jnp.stack([real_gram, mixed], axis=2) * scale).astype(jnp.bfloat16),
        "tm",
        scatter_dimension=0,
        tiled=True,
    ).astype(jnp.float32)
    return (beams, visibilities)

RADIX = 8


def dft_tables(points):
    inner = points // RADIX
    index = np.arange(inner)
    angle = 2.0 * np.pi * (index[:, None] * index[None, :] % inner) / inner
    scale = 1.0 / math.sqrt(points)
    matrix = np.concatenate([np.cos(angle), np.sin(angle)], 1) * scale
    turn = 2.0 * np.pi * (np.arange(RADIX)[:, None] * index[None, :]) / points
    return (
        jnp.asarray(matrix, jnp.bfloat16),
        jnp.asarray(np.cos(turn), jnp.float32),
        jnp.asarray(np.sin(turn), jnp.float32),
    )


def cadd(a, b):
    return a[0] + b[0], a[1] + b[1]


def csub(a, b):
    return a[0] - b[0], a[1] - b[1]


def times_minus_i(a):
    return a[1], -a[0]


def radix4(a):
    s02, d02 = cadd(a[0], a[2]), csub(a[0], a[2])
    s13, d13 = cadd(a[1], a[3]), times_minus_i(csub(a[1], a[3]))
    return [cadd(s02, s13), cadd(d02, d13), csub(s02, s13), csub(d02, d13)]


def radix8(a):
    even, odd = radix4(a[0::2]), radix4(a[1::2])
    root = math.sqrt(0.5)
    o1, o2, o3 = odd[1], times_minus_i(odd[2]), odd[3]
    o1 = ((o1[0] + o1[1]) * root, (o1[1] - o1[0]) * root)
    o3 = ((o3[1] - o3[0]) * root, (-o3[0] - o3[1]) * root)
    odd = [odd[0], o1, o2, o3]
    return [cadd(e, o) for e, o in zip(even, odd)] + [csub(e, o) for e, o in zip(even, odd)]


def first_stage(x_ref, cos_ref, sin_ref, mid):
    _, rows, points = x_ref.shape
    inner = points // RADIX
    chunk = 16

    @pl.loop(0, rows // chunk)
    def _(step):
        at = pl.ds(pl.multiple_of(step * chunk, chunk), chunk)
        low = pl.ds(pl.multiple_of(rows + step * chunk, chunk), chunk)
        for lane in range(0, inner, 128):
            parts = []
            for n1 in range(RADIX):
                cut = pl.ds(n1 * inner + lane, 128)
                parts.append((x_ref[0, at, cut].astype(jnp.float32), x_ref[1, at, cut].astype(jnp.float32)))
            for k1, (re, im) in enumerate(radix8(parts)):
                if k1:
                    c, s = cos_ref[k1:k1 + 1, lane:lane + 128], sin_ref[k1:k1 + 1, lane:lane + 128]
                    re, im = re * c + im * s, im * c - re * s
                re, im = re.astype(jnp.bfloat16), im.astype(jnp.bfloat16)
                left, right = pl.ds(lane, 128), pl.ds(inner + lane, 128)
                mid[k1, at, left] = re
                mid[k1, at, right] = im
                mid[k1, low, left] = im
                mid[k1, low, right] = -re


def second_stage(mid, m_ref, out_ref):
    targets, vch, depth, width = out_ref.shape
    fine = depth // RADIX

    @pl.loop(0, RADIX // 2)
    def _(half):
        pair = mid[pl.ds(2 * half, 2)].reshape(2 * width, mid.shape[2])
        done = lax.dot_general(
            m_ref[...], pair, (((1,), (1,)), ((), ())), preferred_element_type=jnp.float32
        ).astype(jnp.bfloat16)
        for k1 in range(2):
            at = pl.ds(pl.multiple_of((2 * half + k1) * fine, fine), fine)
            out_ref[:, :, at, :] = done[:, k1 * width:(k1 + 1) * width].reshape(targets, vch, fine, width)


def send_order(count):
    near = []
    half = 1
    while half < count // 4:
        near += [(half, j) for j in range(half)]
        half *= 2
    far = [(count // 2, j) for j in range(count // 2)]
    middle = [(half, j) for j in range(half)] if half < count // 2 else []
    mixed = []
    while far or middle:
        mixed += far[:2] + middle[:1]
        far, middle = far[2:], middle[1:]
    return near + mixed


def front_kernel(stat_count, time_count, x_ref, m_ref, cos_ref, sin_ref, w_ref, y_ref, wg_ref,
                 xv, mid, spec, loc, wloc, send, recv, wsend, wrecv, fsend, frecv, keep):
    me, now = lax.axis_index("stat"), lax.axis_index("tm")
    items = spec.shape[0]

    loads = [pltpu.make_async_copy(x_ref.at[:, s], xv.at[s], loc.at[s]) for s in range(items)]
    for load in loads:
        load.start()
    wput = pltpu.make_async_copy(w_ref, wg_ref.at[me], wloc)
    wput.start()

    barrier = pltpu.get_barrier_semaphore()
    for k in range(1, stat_count):
        pl.semaphore_signal(barrier, inc=1, device_id={"stat": lax.rem(me + k, stat_count)},
                            device_id_type=pl.DeviceIdType.MESH)
    for j in range(1, time_count):
        pl.semaphore_signal(barrier, inc=1, device_id={"tm": lax.rem(now + j, time_count)},
                            device_id_type=pl.DeviceIdType.MESH)

    half = stat_count // 2
    far = [(half, j) for j in range(half)]
    near = []
    half //= 2
    while half:
        near = [(half, j) for j in range(half)] + near
        half //= 2
    order = near + far

    def partner(k, sign):
        half = k[0]
        other = me // half + 1 - 2 * lax.rem(me // half, 2)
        return other * half + lax.rem(lax.rem(me, half) + half + sign * k[1], half)

    sends = [partner(k, 1) for k in order]
    sources = [partner(k, -1) for k in order]

    def to(src, dst, there, out_sem, in_sem):
        return pltpu.make_async_remote_copy(
            src_ref=src, dst_ref=dst, send_sem=out_sem, recv_sem=in_sem,
            device_id={"stat": there}, device_id_type=pl.DeviceIdType.MESH)

    ends = []

    def forward(src, s, source, slot):
        for j in range(1, time_count):
            copy = pltpu.make_async_remote_copy(
                src_ref=src, dst_ref=y_ref.at[now, s, source],
                send_sem=fsend.at[s, j, slot], recv_sem=frecv.at[s, j, slot],
                device_id={"tm": lax.rem(now + j, time_count)}, device_id_type=pl.DeviceIdType.MESH)
            copy.start()
            ends.append(copy.wait)

    def issue(s, number):
        there = sends[number]
        copy = to(spec.at[s, there], y_ref.at[now, s, me], there, send.at[s, number], recv.at[s, number])
        copy.start()
        return copy.wait_send

    def own(s):
        forward(spec.at[s, me], s, me, stat_count - 1)
        put = pltpu.make_async_copy(spec.at[s, me], y_ref.at[now, s, me], keep.at[s])
        put.start()
        ends.append(put.wait)

    def take(s, number):
        source = sources[number]
        to(spec.at[s, source], y_ref.at[now, s, source], source, send.at[s, number], recv.at[s, number]).wait_recv()
        forward(y_ref.at[now, s, source], s, source, number)

    levels = []
    reach = stat_count // 2
    while reach:
        levels.append(reach)
        reach //= 2
    started = []

    def start_level():
        level = len(started)
        if level:
            for copy in started[-1]:
                copy.wait_recv()
        reach = levels[level]
        period = 2 * reach
        other = partner((reach, 0), 1)
        made = []
        for turn in range(stat_count // period):
            block = lax.rem(me, period) + period * turn
            index = stat_count // period + turn
            made.append(to(wg_ref.at[block] if level else w_ref, wg_ref.at[block], other,
                           wsend.at[index], wrecv.at[index]))
        for copy in made:
            copy.start()
        started.append(made)

    first = len(near)
    queue = []
    for s in range(items):
        n, f = list(range(first)), list(range(first, first + len(far)))
        for kind in (START if not s else LATER):
            queue.append((s, (n if kind == "n" else f).pop(0)))
        assert not n and not f
    gone = []
    taken = 0
    ready = 0

    def compute(s):
        loads[s].wait()
        first_stage(xv.at[s], cos_ref, sin_ref, mid)
        second_stage(mid, m_ref, spec.at[s])

    compute(0)
    pl.semaphore_wait(barrier, stat_count + time_count - 2)
    own(0)
    for step in range(len(queue) + LAG):
        if step < len(queue):
            s, number = queue[step]
            if step >= WINDOW:
                gone[step - WINDOW]()
            gone.append(issue(s, number))
        if step >= LAG:
            take(*queue[step - LAG])
        if step == 0:
            start_level()
            wput.wait()
        if step in FFTS:
            ready += 1
            compute(ready)
            own(ready)
        if step % 10 == 9 and len(started) < len(levels):
            start_level()
    for wait in gone[len(queue) - WINDOW:]:
        wait()
    while len(started) < len(levels):
        start_level()
    for copy in started[-1]:
        copy.wait_recv()
    for level in started:
        for copy in level:
            copy.wait_send()
    for end in ends:
        end()


START = "nfnnfnfnfnfnfff"
LATER = "fnfnfnfnfnfnfnf"
WINDOW = 6
LAG = 6
FFTS = (4, 8, 12)


def front(voltages, weights, stat_count, time_count, local_vch):
    _, rows, items, points = voltages.shape
    inner = points // RADIX
    dma = pltpu.SemaphoreType.DMA
    width = 2 * rows
    peers = dma((stat_count,))
    each = dma((items, stat_count))
    over = dma((items, time_count, stat_count))
    block = (local_vch, AVG, width)
    matrix, cos_turn, sin_turn = dft_tables(points)
    vmem = pl.BlockSpec(memory_space=pltpu.VMEM)
    hbm = pl.BlockSpec(memory_space=pl.ANY)
    return pl.pallas_call(
        functools.partial(front_kernel, stat_count, time_count),
        in_specs=[hbm, vmem, vmem, vmem, vmem],
        out_specs=[hbm, hbm],
        out_shape=[
            jax.ShapeDtypeStruct((time_count, items, stat_count) + block, jnp.bfloat16),
            jax.ShapeDtypeStruct((stat_count,) + weights.shape, weights.dtype),
        ],
        scratch_shapes=[
            pltpu.VMEM((items, 2, rows, points), jnp.bfloat16),
            pltpu.VMEM((RADIX, width, 2 * inner), jnp.bfloat16),
            pltpu.VMEM((items, stat_count) + block, jnp.bfloat16),
            dma((items,)), dma, each, each, peers, peers, over, over, dma((items,)),
        ],
        compiler_params=pltpu.CompilerParams(
            collective_id=0, has_side_effects=True, vmem_limit_bytes=48 * 1024 * 1024),
        name="front",
    )(voltages.transpose(0, 2, 1, 3), matrix, cos_turn, sin_turn, weights)


def correlate_kernel(scale, now_ref, y_ref, w_ref, beam_ref, vis_ref, cols, left, stacked):
    now = now_ref[0]
    times, items, sources, _, fine, width = y_ref.shape
    depth = items * fine
    total = times * depth
    half = width // 2
    inputs = sources * half
    mine = vis_ref.shape[0]
    groups = vis_ref.shape[2]
    flat = vis_ref.reshape(mine * groups, 128)
    beams = w_ref.shape[2]
    for time in range(times):
        for source in range(0, sources, 2):
            a = y_ref[time, :, source, 0].reshape(depth, width)
            b = y_ref[time, :, source + 1, 0].reshape(depth, width)
            out = pl.ds(source * half, width)
            cols[pl.ds(time * depth, depth), out] = jnp.concatenate([a[:, :half], b[:, :half]], 1)
            cols[pl.ds(total + time * depth, depth), out] = jnp.concatenate([a[:, half:], b[:, half:]], 1)
    for tile in range(0, mine, 128):
        at = pl.ds(pl.multiple_of(now * mine + tile, 128), 128)
        re = (cols[pl.ds(0, total), at]).T
        im = (cols[pl.ds(total, total), at]).T
        left[pl.ds(tile, 128), pl.ds(0, total)] = re
        left[pl.ds(tile, 128), pl.ds(total, total)] = im
        left[pl.ds(mine + tile, 128), pl.ds(0, total)] = im
        left[pl.ds(mine + tile, 128), pl.ds(total, total)] = -re
    block = 256

    @pl.loop(0, inputs // block)
    def _(n):
        at = pl.ds(pl.multiple_of(n * block, block), block)
        for q in range(2):
            value = scale * jnp.dot(
                left[pl.ds(q * mine, mine), :], cols[:, at], preferred_element_type=jnp.float32)
            for part in range(block // 128):
                row = (n * (block // 128) + part) * 2 + q
                flat[pl.ds(row, mine, stride=groups), :] = value[:, part * 128:part * 128 + 128]

    for source in range(sources):
        upper = pl.ds(source * half, half)
        lower = pl.ds(inputs + source * half, half)
        stacked[upper, pl.ds(0, beams)] = w_ref[source, :half]
        stacked[upper, pl.ds(beams, beams)] = w_ref[source, half:]
        stacked[lower, pl.ds(0, beams)] = -w_ref[source, half:]
        stacked[lower, pl.ds(beams, beams)] = w_ref[source, :half]
    shift = pl.multiple_of(now * depth, depth)
    real = jnp.dot(
        cols[pl.ds(shift, depth), :], stacked[pl.ds(0, inputs), :], preferred_element_type=jnp.float32)
    imag = jnp.dot(
        cols[pl.ds(total + shift, depth), :], stacked[pl.ds(inputs, inputs), :],
        preferred_element_type=jnp.float32)
    beam_ref[0] = (real + imag).astype(jnp.bfloat16)


def correlate(spread, weights, now, scale, mine):
    times, items, sources, vch, fine, width = spread.shape
    depth = items * fine
    lanes = sources * width
    wide = 2 * weights.shape[2]
    groups = lanes // 128
    inputs = lanes // 2
    return pl.pallas_call(
        functools.partial(correlate_kernel, scale),
        grid_spec=pltpu.PrefetchScalarGridSpec(
            num_scalar_prefetch=1,
            grid=(vch,),
            in_specs=[
                pl.BlockSpec((times, items, sources, 1, fine, width), lambda v, t: (0, 0, 0, v, 0, 0)),
                pl.BlockSpec(weights.shape, lambda v, t: (0, 0, 0)),
            ],
            out_specs=[
                pl.BlockSpec((1, depth, wide), lambda v, t: (v, 0, 0)),
                pl.BlockSpec((mine, 1, groups, 128), lambda v, t: (0, v, 0, 0)),
            ],
            scratch_shapes=[
                pltpu.VMEM((2 * times * depth, inputs), jnp.bfloat16),
                pltpu.VMEM((2 * mine, 2 * times * depth), jnp.bfloat16),
                pltpu.VMEM((lanes, wide), jnp.bfloat16),
            ],
        ),
        out_shape=[
            jax.ShapeDtypeStruct((vch, depth, wide), jnp.bfloat16),
            jax.ShapeDtypeStruct((mine, vch, groups, 128), jnp.float32),
        ],
        name="correlate",
    )(now, spread, weights)


def fast_body(voltages, beam_weights):
    stat_count = lax.axis_size("stat")
    time_count = lax.axis_size("tm")
    _, rows, items, points = voltages.shape
    beams_count = beam_weights.shape[2]
    local_vch = points // stat_count // AVG
    fine = AVG // RADIX
    width = 2 * rows
    spread, gathered = front(voltages, beam_weights.reshape(width, beams_count), stat_count, time_count, local_vch)
    now = lax.axis_index("tm").astype(jnp.int32).reshape(1)
    scale = 1.0 / (items * time_count * AVG)
    beams, vis = correlate(spread, gathered, now, scale, stat_count * rows // time_count)
    beams = beams.reshape(local_vch, items, RADIX, fine, 2, beams_count).transpose(0, 3, 2, 1, 4, 5)
    beams = beams.reshape(local_vch * AVG, items, 2, beams_count)
    vis = vis.reshape(vis.shape[0], local_vch, -1, 2, 128).transpose(0, 1, 3, 2, 4)
    return beams, vis.reshape(vis.shape[0], local_vch, 2, stat_count * rows)


def fits_tiles(mesh, voltages):
    _, inputs, spectra, points = voltages.shape
    rows = inputs // mesh.shape["stat"]
    mine = inputs // mesh.shape["tm"]
    share = points // mesh.shape["stat"]
    even = mesh.shape["stat"] & (mesh.shape["stat"] - 1) == 0 and mesh.shape["stat"] >= 8
    return even and 2 * rows == 128 and mine % 128 == 0 and share % AVG == 0 and spectra // mesh.shape["tm"] <= 4 and mesh.shape["tm"] <= 2


def solution(mesh):
    def whole(voltages, beam_weights):
        return jax.shard_map(
            fast_body if fits_tiles(mesh, voltages) else body,
            mesh=mesh,
            in_specs=(P(None, "stat", "tm", None), P(None, "stat", None)),
            out_specs=(P("stat", "tm", None, None), P("tm", "stat", None, None)),
            check_vma=False,
        )(voltages, beam_weights)

    return whole
```

```python
import functools
import math

import jax
import jax.numpy as jnp
import numpy as np
from jax import lax
from jax.experimental import pallas as pl
from jax.experimental.pallas import tpu as pltpu
from jax.sharding import PartitionSpec as P

NA = 16
NB = 256
AVG = 128


def dft_block(length):
    index = jnp.arange(length, dtype=jnp.int32)
    product = index[:, None] * index[None, :] % length
    angle = product.astype(jnp.float32) * (2.0 * math.pi / length)
    cosine = jnp.cos(angle)
    sine = jnp.sin(angle)
    return jnp.stack([jnp.stack([cosine, -sine]), jnp.stack([sine, cosine])])


def fine_spectra(voltages):
    block_inputs = voltages.shape[1]
    spectra_count = voltages.shape[2]
    signal = voltages.astype(jnp.float32).reshape(2, block_inputs, spectra_count, NA, NB)
    first = jnp.einsum("poak,pisab->osikb", dft_block(NA), signal, precision=lax.Precision.HIGH)
    outer_index = jnp.arange(NA, dtype=jnp.int32)
    inner_index = jnp.arange(NB, dtype=jnp.int32)
    rotation = (outer_index[:, None] * inner_index[None, :] % (NA * NB)).astype(jnp.float32) * (
        2.0 * math.pi / (NA * NB)
    )
    cos_twist = jnp.cos(rotation)
    sin_twist = jnp.sin(rotation)
    rotated = jnp.stack(
        [first[0] * cos_twist + first[1] * sin_twist, first[1] * cos_twist - first[0] * sin_twist]
    )
    final = jnp.einsum("osikb,ocbq->csiqk", rotated, dft_block(NB), precision=lax.Precision.HIGH)
    norm_factor = 1.0 / math.sqrt(NA * NB)
    return (
        (final * norm_factor).reshape(2, spectra_count, block_inputs, NA * NB).astype(jnp.bfloat16)
    )


def stack_weights(weights):
    return jnp.stack(
        [jnp.stack([weights[0], weights[1]], 1), jnp.stack([-weights[1], weights[0]], 1)], 0
    )


def body(voltages, beam_weights):
    stat_count = lax.axis_size("stat")
    time_count = lax.axis_size("tm")
    block_inputs = voltages.shape[1]
    spectra = fine_spectra(voltages)
    spectra_count = spectra.shape[1]
    channel_share = NA * NB // stat_count
    all_weights = lax.all_gather(beam_weights, "stat", axis=1, tiled=True)
    full_stack = stack_weights(all_weights)
    turned = lax.all_to_all(spectra, "stat", split_axis=3, concat_axis=2, tiled=True)
    item_count = turned.shape[1]

    def add_block(block_index, running):
        offset = (block_index * block_inputs).astype(jnp.int32)
        spec_block = lax.dynamic_slice_in_dim(turned, offset, block_inputs, 2)
        weight_block = lax.dynamic_slice_in_dim(full_stack, offset, block_inputs, 1)
        partial_value = jnp.einsum(
            "psic,piqb->csqb", spec_block, weight_block, preferred_element_type=jnp.float32
        )
        rounded = lax.optimization_barrier(partial_value.astype(jnp.bfloat16))
        return running + rounded.astype(jnp.float32)

    initial = jnp.zeros((turned.shape[3], item_count, 2, beam_weights.shape[2]), jnp.float32)
    beams = lax.fori_loop(0, stat_count, add_block, initial).astype(jnp.bfloat16)
    local_vch = channel_share // AVG
    scale = 1.0 / (spectra_count * time_count * AVG)
    split = turned.reshape(2, spectra_count, stat_count * block_inputs, local_vch, AVG)
    real_gram = jnp.einsum("psiva,psjva->ivj", split, split, preferred_element_type=jnp.float32)
    mixed = jnp.einsum("siva,sjva->ivj", split[1], split[0], preferred_element_type=jnp.float32)
    mixed = mixed - jnp.einsum(
        "siva,sjva->ivj", split[0], split[1], preferred_element_type=jnp.float32
    )
    visibilities = lax.psum_scatter(
        (jnp.stack([real_gram, mixed], axis=2) * scale).astype(jnp.bfloat16),
        "tm",
        scatter_dimension=0,
        tiled=True,
    ).astype(jnp.float32)
    return (beams, visibilities)

RADIX = 8


def dft_tables(points):
    inner = points // RADIX
    index = np.arange(inner)
    angle = 2.0 * np.pi * (index[:, None] * index[None, :] % inner) / inner
    scale = 1.0 / math.sqrt(points)
    matrix = np.concatenate([np.cos(angle), np.sin(angle)], 1) * scale
    turn = 2.0 * np.pi * (np.arange(RADIX)[:, None] * index[None, :]) / points
    return (
        jnp.asarray(matrix, jnp.bfloat16),
        jnp.asarray(np.cos(turn), jnp.float32),
        jnp.asarray(np.sin(turn), jnp.float32),
    )


def cadd(a, b):
    return a[0] + b[0], a[1] + b[1]


def csub(a, b):
    return a[0] - b[0], a[1] - b[1]


def times_minus_i(a):
    return a[1], -a[0]


def radix4(a):
    s02, d02 = cadd(a[0], a[2]), csub(a[0], a[2])
    s13, d13 = cadd(a[1], a[3]), times_minus_i(csub(a[1], a[3]))
    return [cadd(s02, s13), cadd(d02, d13), csub(s02, s13), csub(d02, d13)]


def radix8(a):
    even, odd = radix4(a[0::2]), radix4(a[1::2])
    root = math.sqrt(0.5)
    o1, o2, o3 = odd[1], times_minus_i(odd[2]), odd[3]
    o1 = ((o1[0] + o1[1]) * root, (o1[1] - o1[0]) * root)
    o3 = ((o3[1] - o3[0]) * root, (-o3[0] - o3[1]) * root)
    odd = [odd[0], o1, o2, o3]
    return [cadd(e, o) for e, o in zip(even, odd)] + [csub(e, o) for e, o in zip(even, odd)]


def first_stage(x_ref, cos_ref, sin_ref, mid):
    _, rows, points = x_ref.shape
    inner = points // RADIX
    chunk = 16

    @pl.loop(0, rows // chunk)
    def _(step):
        at = pl.ds(pl.multiple_of(step * chunk, chunk), chunk)
        low = pl.ds(pl.multiple_of(rows + step * chunk, chunk), chunk)
        for lane in range(0, inner, 128):
            parts = []
            for n1 in range(RADIX):
                cut = pl.ds(n1 * inner + lane, 128)
                parts.append((x_ref[0, at, cut].astype(jnp.float32), x_ref[1, at, cut].astype(jnp.float32)))
            for k1, (re, im) in enumerate(radix8(parts)):
                if k1:
                    c, s = cos_ref[k1:k1 + 1, lane:lane + 128], sin_ref[k1:k1 + 1, lane:lane + 128]
                    re, im = re * c + im * s, im * c - re * s
                re, im = re.astype(jnp.bfloat16), im.astype(jnp.bfloat16)
                left, right = pl.ds(lane, 128), pl.ds(inner + lane, 128)
                mid[k1, at, left] = re
                mid[k1, at, right] = im
                mid[k1, low, left] = im
                mid[k1, low, right] = -re


def second_stage(mid, m_ref, out_ref):
    targets, vch, depth, width = out_ref.shape
    fine = depth // RADIX

    @pl.loop(0, RADIX // 2)
    def _(half):
        pair = mid[pl.ds(2 * half, 2)].reshape(2 * width, mid.shape[2])
        done = lax.dot_general(
            m_ref[...], pair, (((1,), (1,)), ((), ())), preferred_element_type=jnp.float32
        ).astype(jnp.bfloat16)
        for k1 in range(2):
            at = pl.ds(pl.multiple_of((2 * half + k1) * fine, fine), fine)
            out_ref[:, :, at, :] = done[:, k1 * width:(k1 + 1) * width].reshape(targets, vch, fine, width)


def near_and_far(count):
    half = count // 2
    far = [(half, j) for j in range(half)]
    near = []
    half //= 2
    while half:
        near = [(half, j) for j in range(half)] + near
        half //= 2
    return near, far


FAR_WINDOW = 5
NEAR_WINDOW = 4
LATE = 3
AHEAD = 2
BLOCK = 256


def gather_columns(now, take, times, sources, cols):
    depth, half = AVG, cols.shape[1] // sources
    total = times * depth
    for time in range(times):
        for source in range(0, sources, 2):
            a, b = take(time, source), take(time, source + 1)
            out = pl.ds(source * half, 2 * half)
            cols[pl.ds(time * depth, depth), out] = jnp.concatenate([a[:, :half], b[:, :half]], 1)
            cols[pl.ds(total + time * depth, depth), out] = jnp.concatenate([a[:, half:], b[:, half:]], 1)


def turn_rows(now, cols, left):
    total = cols.shape[0] // 2
    mine = left.shape[0] // 2
    for tile in range(0, mine, 128):
        at = pl.ds(pl.multiple_of(now * mine + tile, 128), 128)
        re = (cols[pl.ds(0, total), at]).T
        im = (cols[pl.ds(total, total), at]).T
        left[pl.ds(tile, 128), pl.ds(0, total)] = re
        left[pl.ds(tile, 128), pl.ds(total, total)] = im
        left[pl.ds(mine + tile, 128), pl.ds(0, total)] = im
        left[pl.ds(mine + tile, 128), pl.ds(total, total)] = -re


def front_kernel(stat_count, time_count, x_ref, m_ref, cos_ref, sin_ref, w_ref, y_ref, acc_ref, beam_ref,
                 xv, mid, spec, wg, stacked, yb, cols, left, acc, beams,
                 loc, wloc, send, recv, wsend, wrecv, fsend, frecv, keep, fetch, store):
    me, now = lax.axis_index("stat"), lax.axis_index("tm")
    items, _, vch, depth, width = spec.shape
    last = items - 1
    half = width // 2
    mine = left.shape[0] // 2
    inputs = cols.shape[1]
    total = cols.shape[0] // 2
    wide = w_ref.shape[1]

    for s in range(items):
        pltpu.make_async_copy(x_ref.at[:, s], xv.at[s], loc.at[s]).start()
    wput = pltpu.make_async_copy(w_ref, wg.at[me], wloc)
    wput.start()

    barrier = pltpu.get_barrier_semaphore()
    for k in range(1, stat_count):
        pl.semaphore_signal(barrier, inc=1, device_id={"stat": lax.rem(me + k, stat_count)},
                            device_id_type=pl.DeviceIdType.MESH)
    for j in range(1, time_count):
        pl.semaphore_signal(barrier, inc=1, device_id={"tm": lax.rem(now + j, time_count)},
                            device_id_type=pl.DeviceIdType.MESH)

    near, far = near_and_far(stat_count)
    order = near + far
    peers, close = len(order), len(near)

    def partner(k, sign):
        half = k[0]
        other = me // half + 1 - 2 * lax.rem(me // half, 2)
        return other * half + lax.rem(lax.rem(me, half) + half + sign * k[1], half)

    sends = [partner(k, 1) for k in order]
    sources = [partner(k, -1) for k in order]

    def to(src, dst, there, out_sem, in_sem):
        return pltpu.make_async_remote_copy(
            src_ref=src, dst_ref=dst, send_sem=out_sem, recv_sem=in_sem,
            device_id={"stat": there}, device_id_type=pl.DeviceIdType.MESH)

    def forward(src, s, source, slot):
        return [pltpu.make_async_remote_copy(
            src_ref=src, dst_ref=y_ref.at[s, now, source],
            send_sem=fsend.at[s, j, slot], recv_sem=frecv.at[s, j, slot],
            device_id={"tm": lax.rem(now + j, time_count)}, device_id_type=pl.DeviceIdType.MESH)
            for j in range(1, time_count)]

    def issue(s, number):
        there = sends[number]
        return to(spec.at[s, there], y_ref.at[s, now, me], there, send.at[s, number], recv.at[s, number])

    def put(s):
        return pltpu.make_async_copy(spec.at[s, me], y_ref.at[s, now, me], keep.at[s])

    def take(s, number):
        source = sources[number]
        to(spec.at[s, source], y_ref.at[s, now, source], source, send.at[s, number], recv.at[s, number]).wait_recv()
        for copy in forward(y_ref.at[s, now, source], s, source, number):
            copy.start()

    def finish(s):
        put(s).wait()
        for number in range(peers):
            for copy in forward(y_ref.at[s, now, sources[number]], s, sources[number], number):
                copy.wait()
        for copy in forward(spec.at[s, me], s, me, peers):
            copy.wait()

    def transform(s, between=None):
        pltpu.make_async_copy(x_ref.at[:, s], xv.at[s], loc.at[s]).wait()
        first_stage(xv.at[s], cos_ref, sin_ref, mid)
        if between:
            between()
        second_stage(mid, m_ref, spec.at[s])
        for copy in forward(spec.at[s, me], s, me, peers):
            copy.start()
        put(s).start()

    levels = []
    reach = stat_count // 2
    while reach:
        levels.append(reach)
        reach //= 2

    def level_copies(level):
        reach = levels[level]
        period = 2 * reach
        other = partner((reach, 0), 1)
        made = []
        for turn in range(stat_count // period):
            block = lax.rem(me, period) + period * turn
            index = stat_count // period + turn
            made.append(to(wg.at[block] if level else w_ref, wg.at[block], other,
                           wsend.at[index], wrecv.at[index]))
        return made

    def start_level(level):
        if level:
            for copy in level_copies(level - 1):
                copy.wait_recv()
        else:
            wput.wait()
        for copy in level_copies(level):
            copy.start()

    def stack_weights_now():
        for copy in level_copies(len(levels) - 1):
            copy.wait_recv()
        for source in range(stat_count):
            upper = pl.ds(source * half, half)
            lower = pl.ds(inputs + source * half, half)
            stacked[upper, pl.ds(0, wide)] = wg[source, :half]
            stacked[upper, pl.ds(wide, wide)] = wg[source, half:]
            stacked[lower, pl.ds(0, wide)] = -wg[source, half:]
            stacked[lower, pl.ds(wide, wide)] = wg[source, :half]

    def form_beams(s, v, start):
        real = jnp.dot(cols[pl.ds(start, depth), :], stacked[pl.ds(0, inputs), :],
                       preferred_element_type=jnp.float32)
        imag = jnp.dot(cols[pl.ds(total + start, depth), :], stacked[pl.ds(inputs, inputs), :],
                       preferred_element_type=jnp.float32)
        beams[v, s] = (real + imag).astype(jnp.bfloat16)

    def load(s):
        return pltpu.make_async_copy(y_ref.at[s], yb, fetch)

    def add_products(v, n):
        at = pl.ds(n * BLOCK, BLOCK)
        for q in range(2):
            rows = pl.ds(q * mine, mine)
            acc[v, rows, at] += jnp.dot(left[rows, :], cols[:, at], preferred_element_type=jnp.float32)

    def correlate_part(s, part):
        parts = inputs // BLOCK
        if part == 0:
            finish(s)
            load(s).start()
            return
        if part == 1:
            load(s).wait()
        v, n = divmod(part - 1, parts)
        if v >= vch:
            return
        if n == 0:
            gather_columns(now, lambda time, source: yb[time, source, v], time_count, stat_count, cols)
            turn_rows(now, cols, left)
            form_beams(s, v, pl.multiple_of(now * depth, depth))
        add_products(v, n)

    def first_signals():
        pl.semaphore_wait(barrier, stat_count + time_count - 2)
        start_level(0)

    transform(0, first_signals)
    for number in range(close):
        issue(0, number).start()
        if number < FAR_WINDOW:
            issue(0, close + number).start()

    def first_takes():
        for number in range(2):
            take(0, number)
        start_level(1)

    transform(1, first_takes)
    for number in range(NEAR_WINDOW):
        issue(1, number).start()
    for number in range(2, close):
        take(0, number)

    every = 1 + vch * (inputs // BLOCK)
    steps = len(far)
    spots = steps - LATE
    plan = [LATE + min(part * spots // every, spots - 1) for part in range(every)]

    @pl.loop(0, items)
    def _(s):
        for j in range(steps):
            issue(s, close + j).wait_send()
            if j + FAR_WINDOW < steps:
                issue(s, close + j + FAR_WINDOW).start()
            else:
                @pl.when(s < last)
                def _():
                    issue(s + 1, close + j + FAR_WINDOW - steps).start()
            if j < close:
                @pl.when(s < last)
                def _():
                    issue(s + 1, j).wait_send()
                    if j + NEAR_WINDOW < close:
                        issue(s + 1, j + NEAR_WINDOW).start()
                    else:
                        @pl.when(s + 1 < last)
                        def _():
                            issue(s + 2, j + NEAR_WINDOW - close).start()
                    take(s + 1, j)
            take(s, close + j)
            if j % 3 == 2 and j // 3 + 2 < len(levels):
                @pl.when(s == 0)
                def _():
                    start_level(j // 3 + 2)
            if j == AHEAD:
                @pl.when(s + 1 < last)
                def _():
                    transform(s + 2)
            if j == 4:
                @pl.when(s == 0)
                def _():
                    acc[...] = jnp.zeros(acc.shape, acc.dtype)
            if j == 1:
                @pl.when(s == 1)
                def _():
                    stack_weights_now()
            parts = [part for part, spot in enumerate(plan) if spot == j]
            if parts:
                @pl.when(s > 0)
                def _():
                    for part in parts:
                        correlate_part(s - 1, part)

    sent = pltpu.make_async_copy(acc, acc_ref, store.at[0])
    sent.start()
    put(last).wait()
    local = pltpu.make_async_copy(y_ref.at[last, now], yb.at[now], fetch)
    local.start()
    local.wait()
    for v in range(vch):
        gather_columns(now, lambda time, source: yb[now, source, v], 1, stat_count,
                       cols.at[pl.ds(0, 2 * depth)])
        real = jnp.dot(cols[pl.ds(0, depth), :], stacked[pl.ds(0, inputs), :],
                       preferred_element_type=jnp.float32)
        imag = jnp.dot(cols[pl.ds(depth, depth), :], stacked[pl.ds(inputs, inputs), :],
                       preferred_element_type=jnp.float32)
        beams[v, last] = (real + imag).astype(jnp.bfloat16)
    out = pltpu.make_async_copy(beams, beam_ref, store.at[1])
    out.start()
    for number in range(peers):
        for copy in forward(y_ref.at[last, now, sources[number]], last, sources[number], number):
            copy.wait()
    for copy in forward(spec.at[last, me], last, me, peers):
        copy.wait()
    for number in range(close):
        issue(0, number).wait_send()
    for level in range(len(levels)):
        for copy in level_copies(level):
            copy.wait_send()
    sent.wait()
    out.wait()


def front(voltages, weights, stat_count, time_count, local_vch):
    _, rows, items, points = voltages.shape
    inner = points // RADIX
    dma = pltpu.SemaphoreType.DMA
    width = 2 * rows
    inputs = stat_count * rows
    mine = inputs // time_count
    beams = weights.shape[1]
    peers = dma((stat_count,))
    each = dma((items, stat_count))
    over = dma((items, time_count, stat_count))
    block = (local_vch, AVG, width)
    matrix, cos_turn, sin_turn = dft_tables(points)
    vmem = pl.BlockSpec(memory_space=pltpu.VMEM)
    hbm = pl.BlockSpec(memory_space=pl.ANY)
    sums = (local_vch, 2 * mine, inputs)
    formed = (local_vch, items, AVG, 2 * beams)
    return pl.pallas_call(
        functools.partial(front_kernel, stat_count, time_count),
        in_specs=[hbm, vmem, vmem, vmem, vmem],
        out_specs=[hbm, hbm, hbm],
        out_shape=[
            jax.ShapeDtypeStruct((items, time_count, stat_count) + block, jnp.bfloat16),
            jax.ShapeDtypeStruct(sums, jnp.float32),
            jax.ShapeDtypeStruct(formed, jnp.bfloat16),
        ],
        scratch_shapes=[
            pltpu.VMEM((items, 2, rows, points), jnp.bfloat16),
            pltpu.VMEM((RADIX, width, 2 * inner), jnp.bfloat16),
            pltpu.VMEM((items, stat_count) + block, jnp.bfloat16),
            pltpu.VMEM((stat_count,) + weights.shape, weights.dtype),
            pltpu.VMEM((2 * inputs, 2 * beams), jnp.bfloat16),
            pltpu.VMEM((time_count, stat_count) + block, jnp.bfloat16),
            pltpu.VMEM((2 * time_count * AVG, inputs), jnp.bfloat16),
            pltpu.VMEM((2 * mine, 2 * time_count * AVG), jnp.bfloat16),
            pltpu.VMEM(sums, jnp.float32),
            pltpu.VMEM(formed, jnp.bfloat16),
            dma((items,)), dma, each, each, peers, peers, over, over, dma((items,)), dma, dma((2,)),
        ],
        compiler_params=pltpu.CompilerParams(
            collective_id=0, has_side_effects=True, vmem_limit_bytes=52 * 1024 * 1024),
        name="front",
    )(voltages.transpose(0, 2, 1, 3), matrix, cos_turn, sin_turn, weights)


def finish_kernel(scale, now_ref, y_ref, acc_ref, vis_ref, cols, left):
    now = now_ref[0]
    _, times, sources, _, depth, width = y_ref.shape
    mine = vis_ref.shape[0]
    groups = vis_ref.shape[2]
    flat = vis_ref.reshape(mine * groups, 128)
    span = acc_ref.shape[2]
    part_index = pl.program_id(1)

    @pl.when(part_index == 0)
    def _():
        gather_columns(now, lambda time, source: y_ref[0, time, source, 0], times, sources, cols)
        turn_rows(now, cols, left)

    @pl.loop(0, span // BLOCK)
    def _(n):
        here = pl.ds(pl.multiple_of(n * BLOCK, BLOCK), BLOCK)
        at = pl.ds(pl.multiple_of(part_index * span + n * BLOCK, BLOCK), BLOCK)
        for q in range(2):
            rows = pl.ds(q * mine, mine)
            value = scale * (acc_ref[0, rows, here] + jnp.dot(
                left[rows, :], cols[:, at], preferred_element_type=jnp.float32))
            for part in range(BLOCK // 128):
                row = (n * (BLOCK // 128) + part) * 2 + q
                flat[pl.ds(row, mine, stride=groups), :] = value[:, part * 128:part * 128 + 128]


def finish(spread, sums, now, scale):
    items, times, sources, vch, fine, width = spread.shape
    mine = sums.shape[1] // 2
    inputs = sums.shape[2]
    pieces = 2
    groups = 2 * inputs // 128
    return pl.pallas_call(
        functools.partial(finish_kernel, scale),
        grid_spec=pltpu.PrefetchScalarGridSpec(
            num_scalar_prefetch=1,
            grid=(vch, pieces),
            in_specs=[
                pl.BlockSpec((1, times, sources, 1, fine, width), lambda v, h, t: (items - 1, 0, 0, v, 0, 0)),
                pl.BlockSpec((1, 2 * mine, inputs // pieces), lambda v, h, t: (v, 0, h)),
            ],
            out_specs=pl.BlockSpec((mine, 1, groups // pieces, 128), lambda v, h, t: (0, v, h, 0)),
            scratch_shapes=[
                pltpu.VMEM((2 * times * fine, inputs), jnp.bfloat16),
                pltpu.VMEM((2 * mine, 2 * times * fine), jnp.bfloat16),
            ],
        ),
        out_shape=jax.ShapeDtypeStruct((mine, vch, groups, 128), jnp.float32),
        compiler_params=pltpu.CompilerParams(vmem_limit_bytes=60 * 1024 * 1024),
        name="finish",
    )(now, spread, sums)


def fast_body(voltages, beam_weights):
    stat_count = lax.axis_size("stat")
    time_count = lax.axis_size("tm")
    _, rows, items, points = voltages.shape
    beams_count = beam_weights.shape[2]
    local_vch = points // stat_count // AVG
    fine = AVG // RADIX
    width = 2 * rows
    spread, sums, beams = front(
        voltages, beam_weights.reshape(width, beams_count), stat_count, time_count, local_vch)
    now = lax.axis_index("tm").astype(jnp.int32).reshape(1)
    scale = 1.0 / (items * time_count * AVG)
    vis = finish(spread, sums, now, scale)
    beams = beams.reshape(local_vch, items, RADIX, fine, 2, beams_count).transpose(0, 3, 2, 1, 4, 5)
    beams = beams.reshape(local_vch * AVG, items, 2, beams_count)
    vis = vis.reshape(vis.shape[0], local_vch, -1, 2, 128).transpose(0, 1, 3, 2, 4)
    return beams, vis.reshape(vis.shape[0], local_vch, 2, stat_count * rows)


def fits_tiles(mesh, voltages):
    _, inputs, spectra, points = voltages.shape
    rows = inputs // mesh.shape["stat"]
    mine = inputs // mesh.shape["tm"]
    share = points // mesh.shape["stat"]
    even = mesh.shape["stat"] & (mesh.shape["stat"] - 1) == 0 and mesh.shape["stat"] == 16
    return even and 2 * rows == 128 and mine % 128 == 0 and share % AVG == 0 and 2 <= spectra // mesh.shape["tm"] <= 4 and mesh.shape["tm"] == 2


def solution(mesh):
    def whole(voltages, beam_weights):
        return jax.shard_map(
            fast_body if fits_tiles(mesh, voltages) else body,
            mesh=mesh,
            in_specs=(P(None, "stat", "tm", None), P(None, "stat", None)),
            out_specs=(P("stat", "tm", None, None), P("tm", "stat", None, None)),
            check_vma=False,
        )(voltages, beam_weights)

    return whole
```

```python
import functools
import math

import jax
import jax.numpy as jnp
import numpy as np
from jax import lax
from jax.experimental import pallas as pl
from jax.experimental.pallas import tpu as pltpu
from jax.sharding import PartitionSpec as P

NA = 16
NB = 256
AVG = 128


def dft_block(length):
    index = jnp.arange(length, dtype=jnp.int32)
    product = index[:, None] * index[None, :] % length
    angle = product.astype(jnp.float32) * (2.0 * math.pi / length)
    cosine = jnp.cos(angle)
    sine = jnp.sin(angle)
    return jnp.stack([jnp.stack([cosine, -sine]), jnp.stack([sine, cosine])])


def fine_spectra(voltages):
    block_inputs = voltages.shape[1]
    spectra_count = voltages.shape[2]
    signal = voltages.astype(jnp.float32).reshape(2, block_inputs, spectra_count, NA, NB)
    first = jnp.einsum("poak,pisab->osikb", dft_block(NA), signal, precision=lax.Precision.HIGH)
    outer_index = jnp.arange(NA, dtype=jnp.int32)
    inner_index = jnp.arange(NB, dtype=jnp.int32)
    rotation = (outer_index[:, None] * inner_index[None, :] % (NA * NB)).astype(jnp.float32) * (
        2.0 * math.pi / (NA * NB)
    )
    cos_twist = jnp.cos(rotation)
    sin_twist = jnp.sin(rotation)
    rotated = jnp.stack(
        [first[0] * cos_twist + first[1] * sin_twist, first[1] * cos_twist - first[0] * sin_twist]
    )
    final = jnp.einsum("osikb,ocbq->csiqk", rotated, dft_block(NB), precision=lax.Precision.HIGH)
    norm_factor = 1.0 / math.sqrt(NA * NB)
    return (
        (final * norm_factor).reshape(2, spectra_count, block_inputs, NA * NB).astype(jnp.bfloat16)
    )


def stack_weights(weights):
    return jnp.stack(
        [jnp.stack([weights[0], weights[1]], 1), jnp.stack([-weights[1], weights[0]], 1)], 0
    )


def body(voltages, beam_weights):
    stat_count = lax.axis_size("stat")
    time_count = lax.axis_size("tm")
    block_inputs = voltages.shape[1]
    spectra = fine_spectra(voltages)
    spectra_count = spectra.shape[1]
    channel_share = NA * NB // stat_count
    all_weights = lax.all_gather(beam_weights, "stat", axis=1, tiled=True)
    full_stack = stack_weights(all_weights)
    turned = lax.all_to_all(spectra, "stat", split_axis=3, concat_axis=2, tiled=True)
    item_count = turned.shape[1]

    def add_block(block_index, running):
        offset = (block_index * block_inputs).astype(jnp.int32)
        spec_block = lax.dynamic_slice_in_dim(turned, offset, block_inputs, 2)
        weight_block = lax.dynamic_slice_in_dim(full_stack, offset, block_inputs, 1)
        partial_value = jnp.einsum(
            "psic,piqb->csqb", spec_block, weight_block, preferred_element_type=jnp.float32
        )
        rounded = lax.optimization_barrier(partial_value.astype(jnp.bfloat16))
        return running + rounded.astype(jnp.float32)

    initial = jnp.zeros((turned.shape[3], item_count, 2, beam_weights.shape[2]), jnp.float32)
    beams = lax.fori_loop(0, stat_count, add_block, initial).astype(jnp.bfloat16)
    local_vch = channel_share // AVG
    scale = 1.0 / (spectra_count * time_count * AVG)
    split = turned.reshape(2, spectra_count, stat_count * block_inputs, local_vch, AVG)
    real_gram = jnp.einsum("psiva,psjva->ivj", split, split, preferred_element_type=jnp.float32)
    mixed = jnp.einsum("siva,sjva->ivj", split[1], split[0], preferred_element_type=jnp.float32)
    mixed = mixed - jnp.einsum(
        "siva,sjva->ivj", split[0], split[1], preferred_element_type=jnp.float32
    )
    visibilities = lax.psum_scatter(
        (jnp.stack([real_gram, mixed], axis=2) * scale).astype(jnp.bfloat16),
        "tm",
        scatter_dimension=0,
        tiled=True,
    ).astype(jnp.float32)
    return (beams, visibilities)

RADIX = 8


def dft_tables(points):
    inner = points // RADIX
    index = np.arange(inner)
    angle = 2.0 * np.pi * (index[:, None] * index[None, :] % inner) / inner
    scale = 1.0 / math.sqrt(points)
    matrix = np.concatenate([np.cos(angle), np.sin(angle)], 1) * scale
    turn = 2.0 * np.pi * (np.arange(RADIX)[:, None] * index[None, :]) / points
    return (
        jnp.asarray(matrix, jnp.bfloat16),
        jnp.asarray(np.stack([np.cos(turn), np.sin(turn)]), jnp.float32),
    )


def cadd(a, b):
    return a[0] + b[0], a[1] + b[1]


def csub(a, b):
    return a[0] - b[0], a[1] - b[1]


def times_minus_i(a):
    return a[1], -a[0]


def radix4(a):
    s02, d02 = cadd(a[0], a[2]), csub(a[0], a[2])
    s13, d13 = cadd(a[1], a[3]), times_minus_i(csub(a[1], a[3]))
    return [cadd(s02, s13), cadd(d02, d13), csub(s02, s13), csub(d02, d13)]


def radix8(a):
    even, odd = radix4(a[0::2]), radix4(a[1::2])
    root = math.sqrt(0.5)
    o1, o2, o3 = odd[1], times_minus_i(odd[2]), odd[3]
    o1 = ((o1[0] + o1[1]) * root, (o1[1] - o1[0]) * root)
    o3 = ((o3[1] - o3[0]) * root, (-o3[0] - o3[1]) * root)
    odd = [odd[0], o1, o2, o3]
    return [cadd(e, o) for e, o in zip(even, odd)] + [csub(e, o) for e, o in zip(even, odd)]


def first_stage(x_ref, item, items, cos_ref, sin_ref, mid):
    rows = mid.shape[1] // 2
    inner = mid.shape[2] // 2
    held = x_ref.shape[1] // rows
    chunk = 16

    @pl.loop(0, rows // chunk)
    def _(step):
        at = pl.ds(pl.multiple_of(step * chunk, chunk), chunk)
        low = pl.ds(pl.multiple_of(rows + step * chunk, chunk), chunk)
        for lane in range(0, inner, 128):
            parts = []
            for n1 in range(RADIX):
                row = (n1 * inner + lane) // 128 * items + item
                cut = pl.ds(step * chunk * held + row, chunk, stride=held)
                parts.append((x_ref[0, cut, :], x_ref[1, cut, :]))
            for k1, (re, im) in enumerate(radix8(parts)):
                if k1:
                    c, s = cos_ref[k1:k1 + 1, lane:lane + 128], sin_ref[k1:k1 + 1, lane:lane + 128]
                    re, im = re * c + im * s, im * c - re * s
                re, im = re.astype(jnp.bfloat16), im.astype(jnp.bfloat16)
                left, right = pl.ds(lane, 128), pl.ds(inner + lane, 128)
                mid[k1, at, left] = re
                mid[k1, at, right] = im
                mid[k1, low, left] = im
                mid[k1, low, right] = -re


def second_stage(mid, m_ref, out_ref):
    targets, vch, depth, width = out_ref.shape
    fine = depth // RADIX

    @pl.loop(0, RADIX // 2)
    def _(half):
        pair = mid[pl.ds(2 * half, 2)].reshape(2 * width, mid.shape[2])
        done = lax.dot_general(
            m_ref[...], pair, (((1,), (1,)), ((), ())), preferred_element_type=jnp.float32
        ).astype(jnp.bfloat16)
        for k1 in range(2):
            at = pl.ds(pl.multiple_of((2 * half + k1) * fine, fine), fine)
            out_ref[:, :, at, :] = done[:, k1 * width:(k1 + 1) * width].reshape(targets, vch, fine, width)


def near_and_far(count):
    half = count // 2
    far = [(half, j) for j in range(half)]
    near = []
    half //= 2
    while half:
        near = [(half, j) for j in range(half)] + near
        half //= 2
    return near, far


FAR_WINDOW = 5
NEAR_WINDOW = 4
LATE = 3
AHEAD = 2
BLOCK = 256
GROUPS = 4
PIECES = 2


def gather_columns(now, take, times, sources, cols):
    depth, half = AVG, cols.shape[1] // sources
    total = times * depth
    for time in range(times):
        for source in range(0, sources, 2):
            a, b = take(time, source), take(time, source + 1)
            out = pl.ds(source * half, 2 * half)
            cols[pl.ds(time * depth, depth), out] = jnp.concatenate([a[:, :half], b[:, :half]], 1)
            cols[pl.ds(total + time * depth, depth), out] = jnp.concatenate([a[:, half:], b[:, half:]], 1)


def turn_rows(now, cols, left):
    total = cols.shape[0] // 2
    mine = left.shape[0] // 2
    for tile in range(0, mine, 128):
        at = pl.ds(pl.multiple_of(now * mine + tile, 128), 128)
        re = (cols[pl.ds(0, total), at]).T
        im = (cols[pl.ds(total, total), at]).T
        left[pl.ds(tile, 128), pl.ds(0, total)] = re
        left[pl.ds(tile, 128), pl.ds(total, total)] = im
        left[pl.ds(mine + tile, 128), pl.ds(0, total)] = im
        left[pl.ds(mine + tile, 128), pl.ds(total, total)] = -re


def front_kernel(stat_count, time_count, x_ref, m_hbm, turn_hbm, w_hbm, y_ref, acc_ref, beam_ref,
                 m_ref, turn_ref, w_ref, xv, wide_x, mid, spec, wg, stacked, yb, cols, left, acc, beams, lines,
                 const, loc, wloc, send, recv, wsend, wrecv, fsend, frecv, keep, fetch, store):
    me, now = lax.axis_index("stat"), lax.axis_index("tm")
    items, _, vch, depth, width = spec.shape
    last = items - 1
    half = width // 2
    mine = left.shape[0] // 2
    inputs = cols.shape[1]
    total = cols.shape[0] // 2
    wide = w_ref.shape[1]
    cos_ref, sin_ref = turn_ref.at[0], turn_ref.at[1]
    wput = pltpu.make_async_copy(w_ref, wg.at[me], wloc)

    held = x_ref.shape[2]
    group = x_ref.shape[1] // GROUPS
    loads = []
    for c in range(GROUPS):
        at = pl.ds(c * group, group)
        loads.append(pltpu.make_async_copy(x_ref.at[:, at], xv.at[:, at], loc.at[c]))
        loads[-1].start()
    tables = [pltpu.make_async_copy(src, dst, const.at[n])
              for n, (src, dst) in enumerate([(turn_hbm, turn_ref), (w_hbm, w_ref), (m_hbm, m_ref)])]
    for table in tables:
        table.start()

    barrier = pltpu.get_barrier_semaphore()
    for k in range(1, stat_count):
        pl.semaphore_signal(barrier, inc=1, device_id={"stat": lax.rem(me + k, stat_count)},
                            device_id_type=pl.DeviceIdType.MESH)
    for j in range(1, time_count):
        pl.semaphore_signal(barrier, inc=1, device_id={"tm": lax.rem(now + j, time_count)},
                            device_id_type=pl.DeviceIdType.MESH)

    near, far = near_and_far(stat_count)
    order = near + far
    peers, close = len(order), len(near)

    def partner(k, sign):
        half = k[0]
        other = me // half + 1 - 2 * lax.rem(me // half, 2)
        return other * half + lax.rem(lax.rem(me, half) + half + sign * k[1], half)

    sends = [partner(k, 1) for k in order]
    sources = [partner(k, -1) for k in order]

    def to(src, dst, there, out_sem, in_sem):
        return pltpu.make_async_remote_copy(
            src_ref=src, dst_ref=dst, send_sem=out_sem, recv_sem=in_sem,
            device_id={"stat": there}, device_id_type=pl.DeviceIdType.MESH)

    def forward(src, s, source, slot):
        return [pltpu.make_async_remote_copy(
            src_ref=src, dst_ref=y_ref.at[s, now, source],
            send_sem=fsend.at[s, j, slot], recv_sem=frecv.at[s, j, slot],
            device_id={"tm": lax.rem(now + j, time_count)}, device_id_type=pl.DeviceIdType.MESH)
            for j in range(1, time_count)]

    def issue(s, number):
        there = sends[number]
        return to(spec.at[s, there], y_ref.at[s, now, me], there, send.at[s, number], recv.at[s, number])

    def put(s):
        return pltpu.make_async_copy(spec.at[s, me], y_ref.at[s, now, me], keep.at[s])

    def take(s, number):
        source = sources[number]
        to(spec.at[s, source], y_ref.at[s, now, source], source, send.at[s, number], recv.at[s, number]).wait_recv()
        for copy in forward(y_ref.at[s, now, source], s, source, number):
            copy.start()

    def finish(s):
        put(s).wait()
        for number in range(peers):
            for copy in forward(y_ref.at[s, now, sources[number]], s, sources[number], number):
                copy.wait()
        for copy in forward(spec.at[s, me], s, me, peers):
            copy.wait()

    def transform(s, between=None):
        first_stage(wide_x, s, items, cos_ref, sin_ref, mid)
        if between:
            between()
        second_stage(mid, m_ref, spec.at[s])
        for copy in forward(spec.at[s, me], s, me, peers):
            copy.start()
        put(s).start()

    levels = []
    reach = stat_count // 2
    while reach:
        levels.append(reach)
        reach //= 2

    def level_copies(level):
        reach = levels[level]
        period = 2 * reach
        other = partner((reach, 0), 1)
        made = []
        for turn in range(stat_count // period):
            block = lax.rem(me, period) + period * turn
            index = stat_count // period + turn
            made.append(to(wg.at[block] if level else w_ref, wg.at[block], other,
                           wsend.at[index], wrecv.at[index]))
        return made

    def start_level(level):
        if level:
            for copy in level_copies(level - 1):
                copy.wait_recv()
        else:
            wput.wait()
        for copy in level_copies(level):
            copy.start()

    def stack_weights_now():
        for copy in level_copies(len(levels) - 1):
            copy.wait_recv()
        for source in range(stat_count):
            upper = pl.ds(source * half, half)
            lower = pl.ds(inputs + source * half, half)
            stacked[upper, pl.ds(0, wide)] = wg[source, :half]
            stacked[upper, pl.ds(wide, wide)] = wg[source, half:]
            stacked[lower, pl.ds(0, wide)] = -wg[source, half:]
            stacked[lower, pl.ds(wide, wide)] = wg[source, :half]

    lanes = 2 * wide // 128
    fine = depth // RADIX

    def place_beams(s, v, value):
        for k1 in range(RADIX):
            rows = value[k1 * fine:(k1 + 1) * fine]
            for lane in range(lanes):
                q, tile = divmod(lane, lanes // 2)
                start = ((v * depth + k1) * items + s) * lanes + tile * 2 + q
                beams[pl.ds(start, fine, stride=RADIX * items * lanes), :] = rows[:, lane * 128:lane * 128 + 128]

    def form_beams(s, v, start):
        real = jnp.dot(cols[pl.ds(start, depth), :], stacked[pl.ds(0, inputs), :],
                       preferred_element_type=jnp.float32)
        imag = jnp.dot(cols[pl.ds(total + start, depth), :], stacked[pl.ds(inputs, inputs), :],
                       preferred_element_type=jnp.float32)
        place_beams(s, v, real + imag)

    def load(s):
        return pltpu.make_async_copy(y_ref.at[s], yb, fetch)

    def add_products(v, n):
        at = pl.ds(n * BLOCK, BLOCK)
        for q in range(2):
            rows = pl.ds(q * mine, mine)
            acc[v, rows, at] += jnp.dot(left[rows, :], cols[:, at], preferred_element_type=jnp.float32)

    def correlate_part(s, part):
        parts = inputs // BLOCK
        if part == 0:
            finish(s)
            load(s).start()
            return
        if part == 1:
            load(s).wait()
        v, n = divmod(part - 1, parts)
        if v >= vch:
            return
        if n == 0:
            gather_columns(now, lambda time, source: yb[time, source, v], time_count, stat_count, cols)
            turn_rows(now, cols, left)
            form_beams(s, v, pl.multiple_of(now * depth, depth))
        add_products(v, n)

    def first_signals():
        tables[1].wait()
        wput.start()
        pl.semaphore_wait(barrier, stat_count + time_count - 2)
        start_level(0)
        tables[2].wait()

    for c, load_x in enumerate(loads):
        load_x.wait()

        @pl.loop(c * group, (c + 1) * group)
        def _(row):
            at = pl.ds(pl.multiple_of(row * held, held), held)
            for p in range(2):
                wide_x[p, at, :] = xv[p, row].astype(jnp.float32)

    tables[0].wait()
    transform(0, first_signals)
    for number in range(close):
        issue(0, number).start()
        if number < FAR_WINDOW:
            issue(0, close + number).start()

    def first_takes():
        for number in range(2):
            take(0, number)
        start_level(1)

    transform(1, first_takes)
    for number in range(NEAR_WINDOW):
        issue(1, number).start()
    for number in range(2, close):
        take(0, number)

    every = 1 + vch * (inputs // BLOCK)
    steps = len(far)
    spots = steps - LATE
    plan = [LATE + min(part * spots // every, spots - 1) for part in range(every)]

    @pl.loop(0, items)
    def _(s):
        for j in range(steps):
            issue(s, close + j).wait_send()
            if j + FAR_WINDOW < steps:
                issue(s, close + j + FAR_WINDOW).start()
            else:
                @pl.when(s < last)
                def _():
                    issue(s + 1, close + j + FAR_WINDOW - steps).start()
            if j < close:
                @pl.when(s < last)
                def _():
                    issue(s + 1, j).wait_send()
                    if j + NEAR_WINDOW < close:
                        issue(s + 1, j + NEAR_WINDOW).start()
                    else:
                        @pl.when(s + 1 < last)
                        def _():
                            issue(s + 2, j + NEAR_WINDOW - close).start()
                    take(s + 1, j)
            take(s, close + j)
            if j % 3 == 2 and j // 3 + 2 < len(levels):
                @pl.when(s == 0)
                def _():
                    start_level(j // 3 + 2)
            if j == AHEAD:
                @pl.when(s + 1 < last)
                def _():
                    transform(s + 2)
            if j == 4:
                @pl.when(s == 0)
                def _():
                    acc[...] = jnp.zeros(acc.shape, acc.dtype)
            if j == 1:
                @pl.when(s == 1)
                def _():
                    stack_weights_now()
            parts = [part for part, spot in enumerate(plan) if spot == j]
            if parts:
                @pl.when(s > 0)
                def _():
                    for part in parts:
                        correlate_part(s - 1, part)

    sent = pltpu.make_async_copy(acc, acc_ref, store.at[0])
    sent.start()
    put(last).wait()
    local = pltpu.make_async_copy(y_ref.at[last, now], yb.at[now], fetch)
    local.start()
    local.wait()
    for v in range(vch):
        gather_columns(now, lambda time, source: yb[now, source, v], 1, stat_count,
                       cols.at[pl.ds(0, 2 * depth)])
        real = jnp.dot(cols[pl.ds(0, depth), :], stacked[pl.ds(0, inputs), :],
                       preferred_element_type=jnp.float32)
        imag = jnp.dot(cols[pl.ds(depth, depth), :], stacked[pl.ds(inputs, inputs), :],
                       preferred_element_type=jnp.float32)
        place_beams(last, v, real + imag)
    @pl.loop(0, beams.shape[0] // 256)
    def _(n):
        at = pl.ds(pl.multiple_of(n * 256, 256), 256)
        lines[at, :] = beams[at, :].astype(jnp.bfloat16)

    out = pltpu.make_async_copy(lines, beam_ref, store.at[1])
    out.start()
    for number in range(peers):
        for copy in forward(y_ref.at[last, now, sources[number]], last, sources[number], number):
            copy.wait()
    for copy in forward(spec.at[last, me], last, me, peers):
        copy.wait()
    for number in range(close):
        issue(0, number).wait_send()
    for level in range(len(levels)):
        for copy in level_copies(level):
            copy.wait_send()
    sent.wait()
    out.wait()


def front(voltages, weights, stat_count, time_count, local_vch):
    _, rows, items, points = voltages.shape
    inner = points // RADIX
    dma = pltpu.SemaphoreType.DMA
    width = 2 * rows
    inputs = stat_count * rows
    mine = inputs // time_count
    beams = weights.shape[1]
    peers = dma((stat_count,))
    each = dma((items, stat_count))
    over = dma((items, time_count, stat_count))
    block = (local_vch, AVG, width)
    lined = voltages.reshape(2, rows, items, points // 128, 128).transpose(0, 1, 3, 2, 4)
    lined = lined.reshape(2, rows, points // 128 * items, 128)
    matrix, turns = dft_tables(points)
    hbm = pl.BlockSpec(memory_space=pl.ANY)
    sums = (local_vch, 2 * mine, inputs)
    formed = (local_vch * AVG * items * 2 * beams // 128, 128)
    return pl.pallas_call(
        functools.partial(front_kernel, stat_count, time_count),
        in_specs=[pl.BlockSpec(memory_space=pltpu.HBM)] * 4,
        out_specs=[hbm, hbm, hbm],
        out_shape=[
            jax.ShapeDtypeStruct((items, time_count, stat_count) + block, jnp.bfloat16),
            jax.ShapeDtypeStruct(sums, jnp.float32),
            jax.ShapeDtypeStruct(formed, jnp.bfloat16),
        ],
        scratch_shapes=[
            pltpu.VMEM(matrix.shape, matrix.dtype),
            pltpu.VMEM(turns.shape, turns.dtype),
            pltpu.VMEM(weights.shape, weights.dtype),
            pltpu.VMEM(lined.shape, jnp.bfloat16),
            pltpu.VMEM((2, rows * lined.shape[2], 128), jnp.float32),
            pltpu.VMEM((RADIX, width, 2 * inner), jnp.bfloat16),
            pltpu.VMEM((items, stat_count) + block, jnp.bfloat16),
            pltpu.VMEM((stat_count,) + weights.shape, weights.dtype),
            pltpu.VMEM((2 * inputs, 2 * beams), jnp.bfloat16),
            pltpu.VMEM((time_count, stat_count) + block, jnp.bfloat16),
            pltpu.VMEM((2 * time_count * AVG, inputs), jnp.bfloat16),
            pltpu.VMEM((2 * mine, 2 * time_count * AVG), jnp.bfloat16),
            pltpu.VMEM(sums, jnp.float32),
            pltpu.VMEM(formed, jnp.float32),
            pltpu.VMEM(formed, jnp.bfloat16),
            dma((3,)), dma((GROUPS,)), dma, each, each, peers, peers, over, over, dma((items,)), dma, dma((2,)),
        ],
        compiler_params=pltpu.CompilerParams(
            collective_id=0, has_side_effects=True, vmem_limit_bytes=63 * 1024 * 1024),
        name="front",
    )(lined, matrix, turns, weights)


def finish_kernel(scale, now_ref, y_ref, acc_ref, lines_ref, vis_ref, beam_ref, cols, left):
    now = now_ref[0]
    _, times, sources, _, depth, width = y_ref.shape
    mine = vis_ref.shape[0]
    groups = vis_ref.shape[2]
    flat = vis_ref.reshape(mine * groups, 128)
    span = acc_ref.shape[2]
    part_index = pl.program_id(1)
    beam_ref[...] = lines_ref[...]

    @pl.when(part_index == 0)
    def _():
        gather_columns(now, lambda time, source: y_ref[0, time, source, 0], times, sources, cols)
        turn_rows(now, cols, left)

    @pl.loop(0, span // BLOCK)
    def _(n):
        here = pl.ds(pl.multiple_of(n * BLOCK, BLOCK), BLOCK)
        at = pl.ds(pl.multiple_of(part_index * span + n * BLOCK, BLOCK), BLOCK)
        for q in range(2):
            rows = pl.ds(q * mine, mine)
            value = scale * (acc_ref[0, rows, here] + jnp.dot(
                left[rows, :], cols[:, at], preferred_element_type=jnp.float32))
            for part in range(BLOCK // 128):
                row = (n * (BLOCK // 128) + part) * 2 + q
                flat[pl.ds(row, mine, stride=groups), :] = value[:, part * 128:part * 128 + 128]


def finish(spread, sums, lines, now, scale):
    items, times, sources, vch, fine, width = spread.shape
    mine = sums.shape[1] // 2
    inputs = sums.shape[2]
    pieces = PIECES
    share = lines.shape[0] // (vch * pieces)
    some = pl.BlockSpec((share, 128), lambda v, h, t: (v * pieces + h, 0))
    groups = 2 * inputs // 128
    return pl.pallas_call(
        functools.partial(finish_kernel, scale),
        grid_spec=pltpu.PrefetchScalarGridSpec(
            num_scalar_prefetch=1,
            grid=(vch, pieces),
            in_specs=[
                pl.BlockSpec((1, times, sources, 1, fine, width), lambda v, h, t: (items - 1, 0, 0, v, 0, 0)),
                pl.BlockSpec((1, 2 * mine, inputs // pieces), lambda v, h, t: (v, 0, h)),
                some,
            ],
            out_specs=[pl.BlockSpec((mine, 1, groups // pieces, 128), lambda v, h, t: (0, v, h, 0)), some],
            scratch_shapes=[
                pltpu.VMEM((2 * times * fine, inputs), jnp.bfloat16),
                pltpu.VMEM((2 * mine, 2 * times * fine), jnp.bfloat16),
            ],
        ),
        out_shape=[
            jax.ShapeDtypeStruct((mine, vch, groups, 128), jnp.float32),
            jax.ShapeDtypeStruct(lines.shape, lines.dtype),
        ],
        compiler_params=pltpu.CompilerParams(vmem_limit_bytes=63 * 1024 * 1024),
        name="finish",
    )(now, spread, sums, lines)


def fast_body(voltages, beam_weights):
    stat_count = lax.axis_size("stat")
    time_count = lax.axis_size("tm")
    _, rows, items, points = voltages.shape
    beams_count = beam_weights.shape[2]
    local_vch = points // stat_count // AVG
    width = 2 * rows
    spread, sums, beams = front(
        voltages, beam_weights.reshape(width, beams_count), stat_count, time_count, local_vch)
    now = lax.axis_index("tm").astype(jnp.int32).reshape(1)
    scale = 1.0 / (items * time_count * AVG)
    vis, beams = finish(spread, sums, beams, now, scale)
    beams = beams.reshape(local_vch * AVG, items, beams_count // 128, 2, 128).transpose(0, 1, 3, 2, 4)
    beams = beams.reshape(local_vch * AVG, items, 2, beams_count)
    vis = vis.reshape(vis.shape[0], local_vch, -1, 2, 128).transpose(0, 1, 3, 2, 4)
    return beams, vis.reshape(vis.shape[0], local_vch, 2, stat_count * rows)


def fits_tiles(mesh, voltages):
    _, inputs, spectra, points = voltages.shape
    rows = inputs // mesh.shape["stat"]
    mine = inputs // mesh.shape["tm"]
    share = points // mesh.shape["stat"]
    even = mesh.shape["stat"] & (mesh.shape["stat"] - 1) == 0 and mesh.shape["stat"] == 16
    return even and 2 * rows == 128 and mine % 128 == 0 and share % AVG == 0 and 2 <= spectra // mesh.shape["tm"] <= 4 and mesh.shape["tm"] == 2


def solution(mesh):
    def whole(voltages, beam_weights):
        return jax.shard_map(
            fast_body if fits_tiles(mesh, voltages) else body,
            mesh=mesh,
            in_specs=(P(None, "stat", "tm", None), P(None, "stat", None)),
            out_specs=(P("stat", "tm", None, None), P("tm", "stat", None, None)),
            check_vma=False,
        )(voltages, beam_weights)

    return whole
```

```python
import functools
import math

import jax
import jax.numpy as jnp
import numpy as np
from jax import lax
from jax.experimental import pallas as pl
from jax.experimental.pallas import tpu as pltpu
from jax.sharding import PartitionSpec as P

NA = 16
NB = 256
AVG = 128


def dft_block(length):
    index = jnp.arange(length, dtype=jnp.int32)
    product = index[:, None] * index[None, :] % length
    angle = product.astype(jnp.float32) * (2.0 * math.pi / length)
    cosine = jnp.cos(angle)
    sine = jnp.sin(angle)
    return jnp.stack([jnp.stack([cosine, -sine]), jnp.stack([sine, cosine])])


def fine_spectra(voltages):
    block_inputs = voltages.shape[1]
    spectra_count = voltages.shape[2]
    signal = voltages.astype(jnp.float32).reshape(2, block_inputs, spectra_count, NA, NB)
    first = jnp.einsum("poak,pisab->osikb", dft_block(NA), signal, precision=lax.Precision.HIGH)
    outer_index = jnp.arange(NA, dtype=jnp.int32)
    inner_index = jnp.arange(NB, dtype=jnp.int32)
    rotation = (outer_index[:, None] * inner_index[None, :] % (NA * NB)).astype(jnp.float32) * (
        2.0 * math.pi / (NA * NB)
    )
    cos_twist = jnp.cos(rotation)
    sin_twist = jnp.sin(rotation)
    rotated = jnp.stack(
        [first[0] * cos_twist + first[1] * sin_twist, first[1] * cos_twist - first[0] * sin_twist]
    )
    final = jnp.einsum("osikb,ocbq->csiqk", rotated, dft_block(NB), precision=lax.Precision.HIGH)
    norm_factor = 1.0 / math.sqrt(NA * NB)
    return (
        (final * norm_factor).reshape(2, spectra_count, block_inputs, NA * NB).astype(jnp.bfloat16)
    )


def stack_weights(weights):
    return jnp.stack(
        [jnp.stack([weights[0], weights[1]], 1), jnp.stack([-weights[1], weights[0]], 1)], 0
    )


def body(voltages, beam_weights):
    stat_count = lax.axis_size("stat")
    time_count = lax.axis_size("tm")
    block_inputs = voltages.shape[1]
    spectra = fine_spectra(voltages)
    spectra_count = spectra.shape[1]
    channel_share = NA * NB // stat_count
    all_weights = lax.all_gather(beam_weights, "stat", axis=1, tiled=True)
    full_stack = stack_weights(all_weights)
    turned = lax.all_to_all(spectra, "stat", split_axis=3, concat_axis=2, tiled=True)
    item_count = turned.shape[1]

    def add_block(block_index, running):
        offset = (block_index * block_inputs).astype(jnp.int32)
        spec_block = lax.dynamic_slice_in_dim(turned, offset, block_inputs, 2)
        weight_block = lax.dynamic_slice_in_dim(full_stack, offset, block_inputs, 1)
        partial_value = jnp.einsum(
            "psic,piqb->csqb", spec_block, weight_block, preferred_element_type=jnp.float32
        )
        rounded = lax.optimization_barrier(partial_value.astype(jnp.bfloat16))
        return running + rounded.astype(jnp.float32)

    initial = jnp.zeros((turned.shape[3], item_count, 2, beam_weights.shape[2]), jnp.float32)
    beams = lax.fori_loop(0, stat_count, add_block, initial).astype(jnp.bfloat16)
    local_vch = channel_share // AVG
    scale = 1.0 / (spectra_count * time_count * AVG)
    split = turned.reshape(2, spectra_count, stat_count * block_inputs, local_vch, AVG)
    real_gram = jnp.einsum("psiva,psjva->ivj", split, split, preferred_element_type=jnp.float32)
    mixed = jnp.einsum("siva,sjva->ivj", split[1], split[0], preferred_element_type=jnp.float32)
    mixed = mixed - jnp.einsum(
        "siva,sjva->ivj", split[0], split[1], preferred_element_type=jnp.float32
    )
    visibilities = lax.psum_scatter(
        (jnp.stack([real_gram, mixed], axis=2) * scale).astype(jnp.bfloat16),
        "tm",
        scatter_dimension=0,
        tiled=True,
    ).astype(jnp.float32)
    return (beams, visibilities)

RADIX = 8


def dft_tables(points):
    inner = points // RADIX
    index = np.arange(inner)
    angle = 2.0 * np.pi * (index[:, None] * index[None, :] % inner) / inner
    scale = 1.0 / math.sqrt(points)
    matrix = np.concatenate([np.cos(angle), np.sin(angle)], 1) * scale
    turn = 2.0 * np.pi * (np.arange(RADIX)[:, None] * index[None, :]) / points
    return (
        jnp.asarray(matrix, jnp.bfloat16),
        jnp.asarray(np.stack([np.cos(turn), np.sin(turn)]), jnp.float32),
    )


def cadd(a, b):
    return a[0] + b[0], a[1] + b[1]


def csub(a, b):
    return a[0] - b[0], a[1] - b[1]


def times_minus_i(a):
    return a[1], -a[0]


def radix4(a):
    s02, d02 = cadd(a[0], a[2]), csub(a[0], a[2])
    s13, d13 = cadd(a[1], a[3]), times_minus_i(csub(a[1], a[3]))
    return [cadd(s02, s13), cadd(d02, d13), csub(s02, s13), csub(d02, d13)]


def radix8(a):
    even, odd = radix4(a[0::2]), radix4(a[1::2])
    root = math.sqrt(0.5)
    o1, o2, o3 = odd[1], times_minus_i(odd[2]), odd[3]
    o1 = ((o1[0] + o1[1]) * root, (o1[1] - o1[0]) * root)
    o3 = ((o3[1] - o3[0]) * root, (-o3[0] - o3[1]) * root)
    odd = [odd[0], o1, o2, o3]
    return [cadd(e, o) for e, o in zip(even, odd)] + [csub(e, o) for e, o in zip(even, odd)]


def first_stage(x_ref, item, items, cos_ref, sin_ref, mid):
    rows = mid.shape[1] // 2
    inner = mid.shape[2] // 2
    held = x_ref.shape[1] // rows
    chunk = 16

    @pl.loop(0, rows // chunk)
    def _(step):
        at = pl.ds(pl.multiple_of(step * chunk, chunk), chunk)
        low = pl.ds(pl.multiple_of(rows + step * chunk, chunk), chunk)
        for lane in range(0, inner, 128):
            parts = []
            for n1 in range(RADIX):
                row = (n1 * inner + lane) // 128 * items + item
                cut = pl.ds(step * chunk * held + row, chunk, stride=held)
                parts.append((x_ref[0, cut, :], x_ref[1, cut, :]))
            for k1, (re, im) in enumerate(radix8(parts)):
                if k1:
                    c, s = cos_ref[k1:k1 + 1, lane:lane + 128], sin_ref[k1:k1 + 1, lane:lane + 128]
                    re, im = re * c + im * s, im * c - re * s
                re, im = re.astype(jnp.bfloat16), im.astype(jnp.bfloat16)
                left, right = pl.ds(lane, 128), pl.ds(inner + lane, 128)
                mid[k1, at, left] = re
                mid[k1, at, right] = im
                mid[k1, low, left] = im
                mid[k1, low, right] = -re


def second_stage(mid, m_ref, out_ref, part=0, parts=1):
    targets, vch, depth, width = out_ref.shape
    targets //= parts
    some = m_ref.shape[0] // parts
    first = pl.ds(part * targets, targets)
    wanted = pl.ds(part * some, some) if parts == 1 else pl.ds(pl.multiple_of(part * some, 128), some)
    fine = depth // RADIX

    @pl.loop(0, RADIX // 2)
    def _(half):
        pair = mid[pl.ds(2 * half, 2)].reshape(2 * width, mid.shape[2])
        done = lax.dot_general(
            m_ref[wanted, :], pair, (((1,), (1,)), ((), ())), preferred_element_type=jnp.float32
        ).astype(jnp.bfloat16)
        for k1 in range(2):
            at = pl.ds(pl.multiple_of((2 * half + k1) * fine, fine), fine)
            out_ref[first, :, at, :] = done[:, k1 * width:(k1 + 1) * width].reshape(targets, vch, fine, width)


def near_and_far(count):
    half = count // 2
    far = [(half, j) for j in range(half)]
    near = []
    half //= 2
    while half:
        near = [(half, j) for j in range(half)] + near
        half //= 2
    return near, far


FAR_WINDOW = 5
NEAR_WINDOW = 4
LATE = 3
AHEAD = 2
BLOCK = 256
GROUPS = 4
PAD = 8
PIECES = 4


def gather_columns(now, take, times, sources, cols):
    depth, half = AVG, cols.shape[1] // sources
    total = times * depth
    for time in range(times):
        for source in range(0, sources, 2):
            a, b = take(time, source), take(time, source + 1)
            out = pl.ds(source * half, 2 * half)
            cols[pl.ds(time * depth, depth), out] = jnp.concatenate([a[:, :half], b[:, :half]], 1)
            cols[pl.ds(total + time * depth, depth), out] = jnp.concatenate([a[:, half:], b[:, half:]], 1)


def turn_rows(now, cols, left, run=None):
    total = cols.shape[0] // 2
    mine = left.shape[0] // 2
    run = run or mine
    for tile in range(0, mine, 128):
        place = tile // run * 2 * run + tile % run
        at = pl.ds(pl.multiple_of(now * mine + tile, 128), 128)
        re = (cols[pl.ds(0, total), at]).T
        im = (cols[pl.ds(total, total), at]).T
        left[pl.ds(place, 128), pl.ds(0, total)] = re
        left[pl.ds(place, 128), pl.ds(total, total)] = im
        left[pl.ds(place + run, 128), pl.ds(0, total)] = im
        left[pl.ds(place + run, 128), pl.ds(total, total)] = -re


def front_kernel(stat_count, time_count, x_ref, m_hbm, turn_hbm, w_hbm, y_ref, acc_ref, beam_ref,
                 m_ref, turn_ref, w_ref, xv, wide_x, mid, spec, wg, stacked, yb, cols, left, acc, packed, beams, lines,
                 const, loc, wloc, send, recv, wsend, wrecv, fsend, frecv, keep, fetch, store):
    me, now = lax.axis_index("stat"), lax.axis_index("tm")
    items, _, vch, depth, width = spec.shape
    last = items - 1
    half = width // 2
    mine = left.shape[0] // 2
    inputs = cols.shape[1]
    total = cols.shape[0] // 2
    wide = w_ref.shape[1]
    cos_ref, sin_ref = turn_ref.at[0], turn_ref.at[1]
    wput = pltpu.make_async_copy(w_ref, wg.at[me], wloc)

    held = x_ref.shape[2]
    group = x_ref.shape[1] // GROUPS
    loads = []
    for c in range(GROUPS):
        at = pl.ds(c * group, group)
        loads.append(pltpu.make_async_copy(x_ref.at[:, at], xv.at[:, at], loc.at[c]))
        loads[-1].start()
    tables = [pltpu.make_async_copy(src, dst, const.at[n])
              for n, (src, dst) in enumerate([(turn_hbm, turn_ref), (w_hbm, w_ref), (m_hbm, m_ref)])]
    for table in tables:
        table.start()

    barrier = pltpu.get_barrier_semaphore()
    for k in range(1, stat_count):
        pl.semaphore_signal(barrier, inc=1, device_id={"stat": lax.rem(me + k, stat_count)},
                            device_id_type=pl.DeviceIdType.MESH)
    for j in range(1, time_count):
        pl.semaphore_signal(barrier, inc=1, device_id={"tm": lax.rem(now + j, time_count)},
                            device_id_type=pl.DeviceIdType.MESH)

    near, far = near_and_far(stat_count)
    order = near + far
    peers, close = len(order), len(near)

    def partner(k, sign):
        half = k[0]
        other = me // half + 1 - 2 * lax.rem(me // half, 2)
        return other * half + lax.rem(lax.rem(me, half) + half + sign * k[1], half)

    sends = [partner(k, 1) for k in order]
    sources = [partner(k, -1) for k in order]

    def to(src, dst, there, out_sem, in_sem):
        return pltpu.make_async_remote_copy(
            src_ref=src, dst_ref=dst, send_sem=out_sem, recv_sem=in_sem,
            device_id={"stat": there}, device_id_type=pl.DeviceIdType.MESH)

    def forward(src, s, source, slot):
        return [pltpu.make_async_remote_copy(
            src_ref=src, dst_ref=y_ref.at[s, now, source],
            send_sem=fsend.at[s, j, slot], recv_sem=frecv.at[s, j, slot],
            device_id={"tm": lax.rem(now + j, time_count)}, device_id_type=pl.DeviceIdType.MESH)
            for j in range(1, time_count)]

    def issue(s, number):
        there = sends[number]
        return to(spec.at[s, there], y_ref.at[s, now, me], there, send.at[s, number], recv.at[s, number])

    def put(s):
        return pltpu.make_async_copy(spec.at[s, me], y_ref.at[s, now, me], keep.at[s])

    def take(s, number):
        source = sources[number]
        to(spec.at[s, source], y_ref.at[s, now, source], source, send.at[s, number], recv.at[s, number]).wait_recv()
        for copy in forward(y_ref.at[s, now, source], s, source, number):
            copy.start()

    def finish(s):
        put(s).wait()
        for number in range(peers):
            for copy in forward(y_ref.at[s, now, sources[number]], s, sources[number], number):
                copy.wait()
        for copy in forward(spec.at[s, me], s, me, peers):
            copy.wait()

    def own_block(s):
        for copy in forward(spec.at[s, me], s, me, peers):
            copy.start()
        put(s).start()

    def transform(s, between=None):
        first_stage(wide_x, s, items, cos_ref, sin_ref, mid)
        if between:
            between()
        second_stage(mid, m_ref, spec.at[s])
        own_block(s)

    levels = []
    reach = stat_count // 2
    while reach:
        levels.append(reach)
        reach //= 2

    def level_copies(level):
        reach = levels[level]
        period = 2 * reach
        other = partner((reach, 0), 1)
        made = []
        for turn in range(stat_count // period):
            block = lax.rem(me, period) + period * turn
            index = stat_count // period + turn
            made.append(to(wg.at[block] if level else w_ref, wg.at[block], other,
                           wsend.at[index], wrecv.at[index]))
        return made

    def start_level(level):
        if level:
            for copy in level_copies(level - 1):
                copy.wait_recv()
        else:
            wput.wait()
        for copy in level_copies(level):
            copy.start()

    def stack_weights_now():
        for copy in level_copies(len(levels) - 1):
            copy.wait_recv()
        for source in range(stat_count):
            upper = pl.ds(source * half, half)
            lower = pl.ds(inputs + source * half, half)
            stacked[upper, pl.ds(0, wide)] = wg[source, :half]
            stacked[upper, pl.ds(wide, wide)] = wg[source, half:]
            stacked[lower, pl.ds(0, wide)] = -wg[source, half:]
            stacked[lower, pl.ds(wide, wide)] = wg[source, :half]

    lanes = 2 * wide // 128
    fine = depth // RADIX

    def place_beams(s, v, value):
        for k1 in range(RADIX):
            rows = value[k1 * fine:(k1 + 1) * fine]
            for lane in range(lanes):
                q, tile = divmod(lane, lanes // 2)
                start = ((v * depth + k1) * items + s) * lanes + tile * 2 + q
                beams[pl.ds(start, fine, stride=RADIX * items * lanes), :] = rows[:, lane * 128:lane * 128 + 128]

    def form_beams(s, v, start):
        real = jnp.dot(cols[pl.ds(start, depth), :], stacked[pl.ds(0, inputs), :],
                       preferred_element_type=jnp.float32)
        imag = jnp.dot(cols[pl.ds(total + start, depth), :], stacked[pl.ds(inputs, inputs), :],
                       preferred_element_type=jnp.float32)
        place_beams(s, v, real + imag)

    def load(s):
        return pltpu.make_async_copy(y_ref.at[s], yb, fetch)

    def add_products(v, n):
        at = pl.ds(n * BLOCK, BLOCK)
        for q in range(2):
            rows = pl.ds(q * mine, mine)
            value = acc[v, rows, at] + jnp.dot(left[rows, :], cols[:, at], preferred_element_type=jnp.float32)
            acc[v, rows, at] = value
            packed[v, rows, at] = value.astype(packed.dtype)

    def keep_sums(v):
        return pltpu.make_async_copy(packed.at[v], acc_ref.at[v], store.at[1 + v])

    def correlate_part(s, part):
        parts = inputs // BLOCK
        if part == 0:
            finish(s)
            load(s).start()
            return
        if part == 1:
            load(s).wait()
        v, n = divmod(part - 1, parts)
        if v >= vch:
            return
        if n == 0:
            gather_columns(now, lambda time, source: yb[time, source, v], time_count, stat_count, cols)
            turn_rows(now, cols, left)
            form_beams(s, v, pl.multiple_of(now * depth, depth))
        add_products(v, n)
        if n == parts - 1:
            @pl.when(s == last - 1)
            def _():
                keep_sums(v).start()

    for c, load_x in enumerate(loads):
        load_x.wait()

        @pl.loop(c * group, (c + 1) * group)
        def _(row):
            at = pl.ds(pl.multiple_of(row * (held + PAD), 8), held)
            for p in range(2):
                wide_x[p, at, :] = xv[p, row].astype(jnp.float32)

    tables[0].wait()
    first_stage(wide_x, 0, items, cos_ref, sin_ref, mid)
    tables[1].wait()
    wput.start()
    pl.semaphore_wait(barrier, stat_count + time_count - 2)
    start_level(0)
    tables[2].wait()
    away = lax.rem(me // len(far) + 1, 2)
    second_stage(mid, m_ref, spec.at[0], away, 2)
    for number in range(FAR_WINDOW):
        issue(0, close + number).start()
    second_stage(mid, m_ref, spec.at[0], 1 - away, 2)
    own_block(0)
    for number in range(close):
        issue(0, number).start()

    def first_takes():
        for number in range(2):
            take(0, number)
        start_level(1)

    transform(1, first_takes)
    for number in range(NEAR_WINDOW):
        issue(1, number).start()
    for number in range(2, close):
        take(0, number)

    every = 1 + vch * (inputs // BLOCK)
    steps = len(far)
    spots = steps - LATE
    plan = [LATE + min(part * spots // every, spots - 1) for part in range(every)]

    @pl.loop(0, items)
    def _(s):
        for j in range(steps):
            issue(s, close + j).wait_send()
            if j + FAR_WINDOW < steps:
                issue(s, close + j + FAR_WINDOW).start()
            else:
                @pl.when(s < last)
                def _():
                    issue(s + 1, close + j + FAR_WINDOW - steps).start()
            if j < close:
                @pl.when(s < last)
                def _():
                    issue(s + 1, j).wait_send()
                    if j + NEAR_WINDOW < close:
                        issue(s + 1, j + NEAR_WINDOW).start()
                    else:
                        @pl.when(s + 1 < last)
                        def _():
                            issue(s + 2, j + NEAR_WINDOW - close).start()
                    take(s + 1, j)
            take(s, close + j)
            if j % 3 == 2 and j // 3 + 2 < len(levels):
                @pl.when(s == 0)
                def _():
                    start_level(j // 3 + 2)
            if j == AHEAD:
                @pl.when(s + 1 < last)
                def _():
                    transform(s + 2)
            if j == 4:
                @pl.when(s == 0)
                def _():
                    acc[...] = jnp.zeros(acc.shape, acc.dtype)
            if j == 1:
                @pl.when(s == 1)
                def _():
                    stack_weights_now()
            parts = [part for part, spot in enumerate(plan) if spot == j]
            if parts:
                @pl.when(s > 0)
                def _():
                    for part in parts:
                        correlate_part(s - 1, part)

    put(last).wait()
    local = pltpu.make_async_copy(y_ref.at[last, now], yb.at[now], fetch)
    local.start()
    local.wait()
    for v in range(vch):
        gather_columns(now, lambda time, source: yb[now, source, v], 1, stat_count,
                       cols.at[pl.ds(0, 2 * depth)])
        real = jnp.dot(cols[pl.ds(0, depth), :], stacked[pl.ds(0, inputs), :],
                       preferred_element_type=jnp.float32)
        imag = jnp.dot(cols[pl.ds(depth, depth), :], stacked[pl.ds(inputs, inputs), :],
                       preferred_element_type=jnp.float32)
        place_beams(last, v, real + imag)
    @pl.loop(0, beams.shape[0] // 256)
    def _(n):
        at = pl.ds(pl.multiple_of(n * 256, 256), 256)
        lines[at, :] = beams[at, :].astype(jnp.bfloat16)

    out = pltpu.make_async_copy(lines, beam_ref, store.at[0])
    out.start()
    for number in range(peers):
        for copy in forward(y_ref.at[last, now, sources[number]], last, sources[number], number):
            copy.wait()
    for copy in forward(spec.at[last, me], last, me, peers):
        copy.wait()
    for number in range(close):
        issue(0, number).wait_send()
    for level in range(len(levels)):
        for copy in level_copies(level):
            copy.wait_send()
    for v in range(vch):
        keep_sums(v).wait()
    out.wait()


def front(voltages, weights, stat_count, time_count, local_vch):
    _, rows, items, points = voltages.shape
    inner = points // RADIX
    dma = pltpu.SemaphoreType.DMA
    width = 2 * rows
    inputs = stat_count * rows
    mine = inputs // time_count
    beams = weights.shape[1]
    peers = dma((stat_count,))
    each = dma((items, stat_count))
    over = dma((items, time_count, stat_count))
    block = (local_vch, AVG, width)
    lined = voltages.reshape(2, rows, items, points // 128, 128).transpose(0, 1, 3, 2, 4)
    lined = lined.reshape(2, rows, points // 128 * items, 128)
    matrix, turns = dft_tables(points)
    hbm = pl.BlockSpec(memory_space=pl.ANY)
    sums = (local_vch, 2 * mine, inputs)
    formed = (local_vch * AVG * items * 2 * beams // 128, 128)
    return pl.pallas_call(
        functools.partial(front_kernel, stat_count, time_count),
        in_specs=[pl.BlockSpec(memory_space=pltpu.HBM)] * 4,
        out_specs=[hbm, hbm, hbm],
        out_shape=[
            jax.ShapeDtypeStruct((items, time_count, stat_count) + block, jnp.bfloat16),
            jax.ShapeDtypeStruct(sums, jnp.bfloat16),
            jax.ShapeDtypeStruct(formed, jnp.bfloat16),
        ],
        scratch_shapes=[
            pltpu.VMEM(matrix.shape, matrix.dtype),
            pltpu.VMEM(turns.shape, turns.dtype),
            pltpu.VMEM(weights.shape, weights.dtype),
            pltpu.VMEM(lined.shape, jnp.bfloat16),
            pltpu.VMEM((2, rows * (lined.shape[2] + PAD), 128), jnp.float32),
            pltpu.VMEM((RADIX, width, 2 * inner), jnp.bfloat16),
            pltpu.VMEM((items, stat_count) + block, jnp.bfloat16),
            pltpu.VMEM((stat_count,) + weights.shape, weights.dtype),
            pltpu.VMEM((2 * inputs, 2 * beams), jnp.bfloat16),
            pltpu.VMEM((time_count, stat_count) + block, jnp.bfloat16),
            pltpu.VMEM((2 * time_count * AVG, inputs), jnp.bfloat16),
            pltpu.VMEM((2 * mine, 2 * time_count * AVG), jnp.bfloat16),
            pltpu.VMEM(sums, jnp.float32),
            pltpu.VMEM(sums, jnp.bfloat16),
            pltpu.VMEM(formed, jnp.float32),
            pltpu.VMEM(formed, jnp.bfloat16),
            dma((3,)), dma((GROUPS,)), dma, each, each, peers, peers, over, over, dma((items,)), dma, dma((1 + local_vch,)),
        ],
        compiler_params=pltpu.CompilerParams(
            collective_id=0, has_side_effects=True, vmem_limit_bytes=63 * 1024 * 1024),
        name="front",
    )(lined, matrix, turns, weights)


def finish_kernel(scale, y_ref, acc_ref, lines_ref, vis_ref, beam_ref,
                  y, acc, lines, vis, cols, left, take, some, give, pass_on):
    now = lax.axis_index("tm")
    times, sources, vch, depth, width = y.shape
    mine, groups = vis.shape[1], vis.shape[2]
    inputs = cols.shape[1]
    last = y_ref.shape[0] - 1
    run = mine // PIECES

    def ready(v):
        return [pltpu.make_async_copy(y_ref.at[last, :, :, v], y.at[:, :, v], take.at[v]),
                pltpu.make_async_copy(acc_ref.at[v], acc.at[v], some.at[v])]

    for v in range(vch):
        for copy in ready(v):
            copy.start()
    bring = pltpu.make_async_copy(lines_ref, lines, pass_on.at[0])
    bring.start()

    def result(v, step):
        rows = pl.ds(step * run, run)
        return pltpu.make_async_copy(vis.at[v, rows], vis_ref.at[rows, v], give.at[v, step])

    for v in range(vch):
        for copy in ready(v)[:1]:
            copy.wait()
        gather_columns(now, lambda time, source: y[time, source, v], times, sources, cols)
        turn_rows(now, cols, left, run)
        for copy in ready(v)[1:]:
            copy.wait()
        flat = vis.at[v].reshape(mine * groups, 128)

        @pl.loop(0, PIECES)
        def _(step):
            rows = pl.ds(pl.multiple_of(step * 2 * run, 2 * run), 2 * run)
            for n in range(inputs // BLOCK):
                at = pl.ds(n * BLOCK, BLOCK)
                value = jnp.dot(left[rows, :], cols[:, at], preferred_element_type=jnp.float32)
                for q in range(2):
                    mates = pl.ds(pl.multiple_of(q * mine + step * run, run), run)
                    whole = scale * (acc[v, mates, at].astype(jnp.float32) + value[q * run:(q + 1) * run])
                    for part in range(BLOCK // 128):
                        row = step * run * groups + (n * (BLOCK // 128) + part) * 2 + q
                        flat[pl.ds(row, run, stride=groups), :] = whole[:, part * 128:part * 128 + 128]
            result(v, step).start()

        if v == 0:
            bring.wait()
            hand = pltpu.make_async_copy(lines, beam_ref, pass_on.at[1])
            hand.start()
    for v in range(vch):
        for step in range(PIECES):
            result(v, step).wait()
    hand.wait()


def finish(spread, sums, lines, scale):
    _, times, sources, vch, fine, width = spread.shape
    mine = sums.shape[1] // 2
    inputs = sums.shape[2]
    groups = 2 * inputs // 128
    dma = pltpu.SemaphoreType.DMA
    hbm = pl.BlockSpec(memory_space=pl.ANY)
    return pl.pallas_call(
        functools.partial(finish_kernel, scale),
        in_specs=[hbm] * 3,
        out_specs=[hbm] * 2,
        scratch_shapes=[
            pltpu.VMEM(spread.shape[1:], spread.dtype),
            pltpu.VMEM(sums.shape, sums.dtype),
            pltpu.VMEM(lines.shape, lines.dtype),
            pltpu.VMEM((vch, mine, groups, 128), jnp.float32),
            pltpu.VMEM((2 * times * fine, inputs), jnp.bfloat16),
            pltpu.VMEM((2 * mine, 2 * times * fine), jnp.bfloat16),
            dma((vch,)), dma((vch,)), dma((vch, PIECES)), dma((2,)),
        ],
        out_shape=[
            jax.ShapeDtypeStruct((mine, vch, groups, 128), jnp.float32),
            jax.ShapeDtypeStruct(lines.shape, lines.dtype),
        ],
        compiler_params=pltpu.CompilerParams(vmem_limit_bytes=63 * 1024 * 1024),
        name="finish",
    )(spread, sums, lines)


def fast_body(voltages, beam_weights):
    stat_count = lax.axis_size("stat")
    time_count = lax.axis_size("tm")
    _, rows, items, points = voltages.shape
    beams_count = beam_weights.shape[2]
    local_vch = points // stat_count // AVG
    width = 2 * rows
    spread, sums, beams = front(
        voltages, beam_weights.reshape(width, beams_count), stat_count, time_count, local_vch)
    scale = 1.0 / (items * time_count * AVG)
    vis, beams = finish(spread, sums, beams, scale)
    beams = beams.reshape(local_vch * AVG, items, beams_count // 128, 2, 128).transpose(0, 1, 3, 2, 4)
    beams = beams.reshape(local_vch * AVG, items, 2, beams_count)
    vis = vis.reshape(vis.shape[0], local_vch, -1, 2, 128).transpose(0, 1, 3, 2, 4)
    return beams, vis.reshape(vis.shape[0], local_vch, 2, stat_count * rows)


def fits_tiles(mesh, voltages):
    _, inputs, spectra, points = voltages.shape
    rows = inputs // mesh.shape["stat"]
    mine = inputs // mesh.shape["tm"]
    share = points // mesh.shape["stat"]
    even = mesh.shape["stat"] & (mesh.shape["stat"] - 1) == 0 and mesh.shape["stat"] == 16
    return even and 2 * rows == 128 and mine % 128 == 0 and share % AVG == 0 and 2 <= spectra // mesh.shape["tm"] <= 4 and mesh.shape["tm"] == 2


def solution(mesh):
    def whole(voltages, beam_weights):
        return jax.shard_map(
            fast_body if fits_tiles(mesh, voltages) else body,
            mesh=mesh,
            in_specs=(P(None, "stat", "tm", None), P(None, "stat", None)),
            out_specs=(P("stat", "tm", None, None), P("tm", "stat", None, None)),
            check_vma=False,
        )(voltages, beam_weights)

    return whole
```

```python
import functools
import math

import jax
import jax.numpy as jnp
import numpy as np
from jax import lax
from jax.experimental import pallas as pl
from jax.experimental.pallas import tpu as pltpu
from jax.sharding import PartitionSpec as P

NA = 16
NB = 256
AVG = 128


def dft_block(length):
    index = jnp.arange(length, dtype=jnp.int32)
    product = index[:, None] * index[None, :] % length
    angle = product.astype(jnp.float32) * (2.0 * math.pi / length)
    cosine = jnp.cos(angle)
    sine = jnp.sin(angle)
    return jnp.stack([jnp.stack([cosine, -sine]), jnp.stack([sine, cosine])])


def fine_spectra(voltages):
    block_inputs = voltages.shape[1]
    spectra_count = voltages.shape[2]
    signal = voltages.astype(jnp.float32).reshape(2, block_inputs, spectra_count, NA, NB)
    first = jnp.einsum("poak,pisab->osikb", dft_block(NA), signal, precision=lax.Precision.HIGH)
    outer_index = jnp.arange(NA, dtype=jnp.int32)
    inner_index = jnp.arange(NB, dtype=jnp.int32)
    rotation = (outer_index[:, None] * inner_index[None, :] % (NA * NB)).astype(jnp.float32) * (
        2.0 * math.pi / (NA * NB)
    )
    cos_twist = jnp.cos(rotation)
    sin_twist = jnp.sin(rotation)
    rotated = jnp.stack(
        [first[0] * cos_twist + first[1] * sin_twist, first[1] * cos_twist - first[0] * sin_twist]
    )
    final = jnp.einsum("osikb,ocbq->csiqk", rotated, dft_block(NB), precision=lax.Precision.HIGH)
    norm_factor = 1.0 / math.sqrt(NA * NB)
    return (
        (final * norm_factor).reshape(2, spectra_count, block_inputs, NA * NB).astype(jnp.bfloat16)
    )


def stack_weights(weights):
    return jnp.stack(
        [jnp.stack([weights[0], weights[1]], 1), jnp.stack([-weights[1], weights[0]], 1)], 0
    )


def body(voltages, beam_weights):
    stat_count = lax.axis_size("stat")
    time_count = lax.axis_size("tm")
    block_inputs = voltages.shape[1]
    spectra = fine_spectra(voltages)
    spectra_count = spectra.shape[1]
    channel_share = NA * NB // stat_count
    all_weights = lax.all_gather(beam_weights, "stat", axis=1, tiled=True)
    full_stack = stack_weights(all_weights)
    turned = lax.all_to_all(spectra, "stat", split_axis=3, concat_axis=2, tiled=True)
    item_count = turned.shape[1]

    def add_block(block_index, running):
        offset = (block_index * block_inputs).astype(jnp.int32)
        spec_block = lax.dynamic_slice_in_dim(turned, offset, block_inputs, 2)
        weight_block = lax.dynamic_slice_in_dim(full_stack, offset, block_inputs, 1)
        partial_value = jnp.einsum(
            "psic,piqb->csqb", spec_block, weight_block, preferred_element_type=jnp.float32
        )
        rounded = lax.optimization_barrier(partial_value.astype(jnp.bfloat16))
        return running + rounded.astype(jnp.float32)

    initial = jnp.zeros((turned.shape[3], item_count, 2, beam_weights.shape[2]), jnp.float32)
    beams = lax.fori_loop(0, stat_count, add_block, initial).astype(jnp.bfloat16)
    local_vch = channel_share // AVG
    scale = 1.0 / (spectra_count * time_count * AVG)
    split = turned.reshape(2, spectra_count, stat_count * block_inputs, local_vch, AVG)
    real_gram = jnp.einsum("psiva,psjva->ivj", split, split, preferred_element_type=jnp.float32)
    mixed = jnp.einsum("siva,sjva->ivj", split[1], split[0], preferred_element_type=jnp.float32)
    mixed = mixed - jnp.einsum(
        "siva,sjva->ivj", split[0], split[1], preferred_element_type=jnp.float32
    )
    visibilities = lax.psum_scatter(
        (jnp.stack([real_gram, mixed], axis=2) * scale).astype(jnp.bfloat16),
        "tm",
        scatter_dimension=0,
        tiled=True,
    ).astype(jnp.float32)
    return (beams, visibilities)

RADIX = 8


def dft_tables(points):
    inner = points // RADIX
    index = np.arange(inner)
    angle = 2.0 * np.pi * (index[:, None] * index[None, :] % inner) / inner
    scale = 1.0 / math.sqrt(points)
    matrix = np.concatenate([np.cos(angle), np.sin(angle)], 1) * scale
    turn = 2.0 * np.pi * (np.arange(RADIX)[:, None] * index[None, :]) / points
    return (
        jnp.asarray(matrix, jnp.bfloat16),
        jnp.asarray(np.stack([np.cos(turn), np.sin(turn)]), jnp.float32),
    )


def cadd(a, b):
    return a[0] + b[0], a[1] + b[1]


def csub(a, b):
    return a[0] - b[0], a[1] - b[1]


def times_minus_i(a):
    return a[1], -a[0]


def radix4(a):
    s02, d02 = cadd(a[0], a[2]), csub(a[0], a[2])
    s13, d13 = cadd(a[1], a[3]), times_minus_i(csub(a[1], a[3]))
    return [cadd(s02, s13), cadd(d02, d13), csub(s02, s13), csub(d02, d13)]


def radix8(a):
    even, odd = radix4(a[0::2]), radix4(a[1::2])
    root = math.sqrt(0.5)
    o1, o2, o3 = odd[1], times_minus_i(odd[2]), odd[3]
    o1 = ((o1[0] + o1[1]) * root, (o1[1] - o1[0]) * root)
    o3 = ((o3[1] - o3[0]) * root, (-o3[0] - o3[1]) * root)
    odd = [odd[0], o1, o2, o3]
    return [cadd(e, o) for e, o in zip(even, odd)] + [csub(e, o) for e, o in zip(even, odd)]


def first_stage(x_ref, item, items, cos_ref, sin_ref, mid):
    rows = mid.shape[1] // 2
    inner = mid.shape[2] // 2
    held = x_ref.shape[1] // rows
    chunk = 16

    @pl.loop(0, rows // chunk)
    def _(step):
        at = pl.ds(pl.multiple_of(step * chunk, chunk), chunk)
        low = pl.ds(pl.multiple_of(rows + step * chunk, chunk), chunk)
        for lane in range(0, inner, 128):
            parts = []
            for n1 in range(RADIX):
                row = (n1 * inner + lane) // 128 * items + item
                cut = pl.ds(step * chunk * held + row, chunk, stride=held)
                parts.append((x_ref[0, cut, :], x_ref[1, cut, :]))
            for k1, (re, im) in enumerate(radix8(parts)):
                if k1:
                    c, s = cos_ref[k1:k1 + 1, lane:lane + 128], sin_ref[k1:k1 + 1, lane:lane + 128]
                    re, im = re * c + im * s, im * c - re * s
                re, im = re.astype(jnp.bfloat16), im.astype(jnp.bfloat16)
                left, right = pl.ds(lane, 128), pl.ds(inner + lane, 128)
                mid[k1, at, left] = re
                mid[k1, at, right] = im
                mid[k1, low, left] = im
                mid[k1, low, right] = -re


def second_stage(mid, m_ref, out_ref, part=0, parts=1):
    targets, vch, depth, width = out_ref.shape
    targets //= parts
    some = m_ref.shape[0] // parts
    first = pl.ds(part * targets, targets)
    wanted = pl.ds(part * some, some) if parts == 1 else pl.ds(pl.multiple_of(part * some, 128), some)
    fine = depth // RADIX

    @pl.loop(0, RADIX // 2)
    def _(half):
        pair = mid[pl.ds(2 * half, 2)].reshape(2 * width, mid.shape[2])
        done = lax.dot_general(
            m_ref[wanted, :], pair, (((1,), (1,)), ((), ())), preferred_element_type=jnp.float32
        ).astype(jnp.bfloat16)
        for k1 in range(2):
            at = pl.ds(pl.multiple_of((2 * half + k1) * fine, fine), fine)
            out_ref[first, :, at, :] = done[:, k1 * width:(k1 + 1) * width].reshape(targets, vch, fine, width)


def near_and_far(count):
    half = count // 2
    far = [(half, (j // 2 + j % 2 * (half // 2)) % half) for j in range(half)]
    near = []
    half //= 2
    while half:
        near = [(half, j) for j in range(half)] + near
        half //= 2
    return near, far


FAR_WINDOW = 5
NEAR_WINDOW = 4
LATE = 3
AHEAD = 2
BLOCK = 256
GROUPS = 4
PAD = 8
PIECES = 4


def gather_columns(now, take, times, sources, cols):
    depth, half = AVG, cols.shape[1] // sources
    total = times * depth
    for time in range(times):
        for source in range(0, sources, 2):
            a, b = take(time, source), take(time, source + 1)
            out = pl.ds(source * half, 2 * half)
            cols[pl.ds(time * depth, depth), out] = jnp.concatenate([a[:, :half], b[:, :half]], 1)
            cols[pl.ds(total + time * depth, depth), out] = jnp.concatenate([a[:, half:], b[:, half:]], 1)


def turn_rows(now, cols, left, run=None):
    total = cols.shape[0] // 2
    mine = left.shape[0] // 2
    run = run or mine
    for tile in range(0, mine, 128):
        place = tile // run * 2 * run + tile % run
        at = pl.ds(pl.multiple_of(now * mine + tile, 128), 128)
        re = (cols[pl.ds(0, total), at]).T
        im = (cols[pl.ds(total, total), at]).T
        left[pl.ds(place, 128), pl.ds(0, total)] = re
        left[pl.ds(place, 128), pl.ds(total, total)] = im
        left[pl.ds(place + run, 128), pl.ds(0, total)] = im
        left[pl.ds(place + run, 128), pl.ds(total, total)] = -re


def front_kernel(stat_count, time_count, x_ref, m_hbm, turn_hbm, w_hbm, y_ref, acc_ref, beam_ref,
                 m_ref, turn_ref, w_ref, xv, wide_x, mid, spec, wg, stacked, yb, cols, left, acc, packed, beams, lines,
                 const, loc, wloc, send, recv, wsend, wrecv, fsend, frecv, keep, fetch, store):
    me, now = lax.axis_index("stat"), lax.axis_index("tm")
    items, _, vch, depth, width = spec.shape
    last = items - 1
    half = width // 2
    mine = left.shape[0] // 2
    inputs = cols.shape[1]
    total = cols.shape[0] // 2
    wide = w_ref.shape[1]
    cos_ref, sin_ref = turn_ref.at[0], turn_ref.at[1]
    wput = pltpu.make_async_copy(w_ref, wg.at[me], wloc)

    barrier = pltpu.get_barrier_semaphore()
    for k in range(1, stat_count):
        pl.semaphore_signal(barrier, inc=1, device_id={"stat": lax.rem(me + k, stat_count)},
                            device_id_type=pl.DeviceIdType.MESH)
    for j in range(1, time_count):
        pl.semaphore_signal(barrier, inc=1, device_id={"tm": lax.rem(now + j, time_count)},
                            device_id_type=pl.DeviceIdType.MESH)

    held = x_ref.shape[2]
    group = x_ref.shape[1] // GROUPS
    tables = [pltpu.make_async_copy(src, dst, const.at[n])
              for n, (src, dst) in enumerate([(turn_hbm, turn_ref), (w_hbm, w_ref), (m_hbm, m_ref)])]
    tables[1].start()
    loads = []
    for c in range(GROUPS):
        at = pl.ds(c * group, group)
        loads.append(pltpu.make_async_copy(x_ref.at[:, at], xv.at[:, at], loc.at[c]))
        loads[-1].start()
    tables[0].start()
    tables[2].start()

    near, far = near_and_far(stat_count)
    order = near + far
    peers, close = len(order), len(near)

    def partner(k, sign):
        half = k[0]
        other = me // half + 1 - 2 * lax.rem(me // half, 2)
        return other * half + lax.rem(lax.rem(me, half) + half + sign * k[1], half)

    sends = [partner(k, 1) for k in order]
    sources = [partner(k, -1) for k in order]

    def to(src, dst, there, out_sem, in_sem):
        return pltpu.make_async_remote_copy(
            src_ref=src, dst_ref=dst, send_sem=out_sem, recv_sem=in_sem,
            device_id={"stat": there}, device_id_type=pl.DeviceIdType.MESH)

    def forward(src, s, source, slot):
        return [pltpu.make_async_remote_copy(
            src_ref=src, dst_ref=y_ref.at[s, now, source],
            send_sem=fsend.at[s, j, slot], recv_sem=frecv.at[s, j, slot],
            device_id={"tm": lax.rem(now + j, time_count)}, device_id_type=pl.DeviceIdType.MESH)
            for j in range(1, time_count)]

    def issue(s, number):
        there = sends[number]
        return to(spec.at[s, there], y_ref.at[s, now, me], there, send.at[s, number], recv.at[s, number])

    def put(s):
        return pltpu.make_async_copy(spec.at[s, me], y_ref.at[s, now, me], keep.at[s])

    def take(s, number):
        source = sources[number]
        to(spec.at[s, source], y_ref.at[s, now, source], source, send.at[s, number], recv.at[s, number]).wait_recv()
        for copy in forward(y_ref.at[s, now, source], s, source, number):
            copy.start()

    def finish(s):
        put(s).wait()
        for number in range(peers):
            for copy in forward(y_ref.at[s, now, sources[number]], s, sources[number], number):
                copy.wait()
        for copy in forward(spec.at[s, me], s, me, peers):
            copy.wait()

    def own_block(s):
        for copy in forward(spec.at[s, me], s, me, peers):
            copy.start()
        put(s).start()

    def transform(s, between=None):
        first_stage(wide_x, s, items, cos_ref, sin_ref, mid)
        if between:
            between()
        second_stage(mid, m_ref, spec.at[s])
        own_block(s)

    levels = []
    reach = stat_count // 2
    while reach:
        levels.append(reach)
        reach //= 2

    def level_copies(level):
        reach = levels[level]
        period = 2 * reach
        other = partner((reach, 0), 1)
        made = []
        for turn in range(stat_count // period):
            block = lax.rem(me, period) + period * turn
            index = stat_count // period + turn
            made.append(to(wg.at[block] if level else w_ref, wg.at[block], other,
                           wsend.at[index], wrecv.at[index]))
        return made

    def start_level(level):
        if level:
            for copy in level_copies(level - 1):
                copy.wait_recv()
        else:
            wput.wait()
        for copy in level_copies(level):
            copy.start()

    def stack_weights_now():
        for copy in level_copies(len(levels) - 1):
            copy.wait_recv()
        for source in range(stat_count):
            upper = pl.ds(source * half, half)
            lower = pl.ds(inputs + source * half, half)
            stacked[upper, pl.ds(0, wide)] = wg[source, :half]
            stacked[upper, pl.ds(wide, wide)] = wg[source, half:]
            stacked[lower, pl.ds(0, wide)] = -wg[source, half:]
            stacked[lower, pl.ds(wide, wide)] = wg[source, :half]

    lanes = 2 * wide // 128
    fine = depth // RADIX

    def place_beams(s, v, value):
        for k1 in range(RADIX):
            rows = value[k1 * fine:(k1 + 1) * fine]
            for lane in range(lanes):
                q, tile = divmod(lane, lanes // 2)
                start = ((v * depth + k1) * items + s) * lanes + tile * 2 + q
                beams[pl.ds(start, fine, stride=RADIX * items * lanes), :] = rows[:, lane * 128:lane * 128 + 128]

    def form_beams(s, v, start):
        real = jnp.dot(cols[pl.ds(start, depth), :], stacked[pl.ds(0, inputs), :],
                       preferred_element_type=jnp.float32)
        imag = jnp.dot(cols[pl.ds(total + start, depth), :], stacked[pl.ds(inputs, inputs), :],
                       preferred_element_type=jnp.float32)
        place_beams(s, v, real + imag)

    def load(s):
        return pltpu.make_async_copy(y_ref.at[s], yb, fetch)

    def add_products(v, n):
        at = pl.ds(n * BLOCK, BLOCK)
        for q in range(2):
            rows = pl.ds(q * mine, mine)
            value = acc[v, rows, at] + jnp.dot(left[rows, :], cols[:, at], preferred_element_type=jnp.float32)
            acc[v, rows, at] = value
            packed[v, rows, at] = value.astype(packed.dtype)

    def keep_sums(v):
        return pltpu.make_async_copy(packed.at[v], acc_ref.at[v], store.at[1 + v])

    def correlate_part(s, part):
        parts = inputs // BLOCK
        if part == 0:
            finish(s)
            load(s).start()
            return
        if part == 1:
            load(s).wait()
        v, n = divmod(part - 1, parts)
        if v >= vch:
            return
        if n == 0:
            gather_columns(now, lambda time, source: yb[time, source, v], time_count, stat_count, cols)
            turn_rows(now, cols, left)
            form_beams(s, v, pl.multiple_of(now * depth, depth))
        add_products(v, n)
        if n == parts - 1:
            @pl.when(s == last - 1)
            def _():
                keep_sums(v).start()

    for c, load_x in enumerate(loads):
        load_x.wait()

        @pl.loop(c * group, (c + 1) * group)
        def _(row):
            at = pl.ds(pl.multiple_of(row * (held + PAD), 8), held)
            for p in range(2):
                wide_x[p, at, :] = xv[p, row].astype(jnp.float32)

    tables[1].wait()
    wput.start()
    pl.semaphore_wait(barrier, stat_count + time_count - 2)
    start_level(0)
    tables[0].wait()
    first_stage(wide_x, 0, items, cos_ref, sin_ref, mid)
    tables[2].wait()
    away = lax.rem(me // len(far) + 1, 2)
    second_stage(mid, m_ref, spec.at[0], away, 2)
    for number in range(FAR_WINDOW):
        issue(0, close + number).start()
    second_stage(mid, m_ref, spec.at[0], 1 - away, 2)
    own_block(0)
    for number in range(close):
        issue(0, number).start()

    def first_takes():
        for number in range(2):
            take(0, number)
        start_level(1)

    transform(1, first_takes)
    for number in range(NEAR_WINDOW):
        issue(1, number).start()
    for number in range(2, close):
        take(0, number)

    every = 1 + vch * (inputs // BLOCK)
    steps = len(far)
    spots = steps - LATE
    plan = [LATE + min(part * spots // every, spots - 1) for part in range(every)]

    @pl.loop(0, items)
    def _(s):
        for j in range(steps):
            issue(s, close + j).wait_send()
            if j + FAR_WINDOW < steps:
                issue(s, close + j + FAR_WINDOW).start()
            else:
                @pl.when(s < last)
                def _():
                    issue(s + 1, close + j + FAR_WINDOW - steps).start()
            if j < close:
                @pl.when(s < last)
                def _():
                    issue(s + 1, j).wait_send()
                    if j + NEAR_WINDOW < close:
                        issue(s + 1, j + NEAR_WINDOW).start()
                    else:
                        @pl.when(s + 1 < last)
                        def _():
                            issue(s + 2, j + NEAR_WINDOW - close).start()
                    take(s + 1, j)
            take(s, close + j)
            if j % 3 == 2 and j // 3 + 2 < len(levels):
                @pl.when(s == 0)
                def _():
                    start_level(j // 3 + 2)
            if j == AHEAD:
                @pl.when(s + 1 < last)
                def _():
                    transform(s + 2)
            if j == 4:
                @pl.when(s == 0)
                def _():
                    acc[...] = jnp.zeros(acc.shape, acc.dtype)
            if j == 1:
                @pl.when(s == 1)
                def _():
                    stack_weights_now()
            parts = [part for part, spot in enumerate(plan) if spot == j]
            if parts:
                @pl.when(s > 0)
                def _():
                    for part in parts:
                        correlate_part(s - 1, part)

    put(last).wait()
    local = pltpu.make_async_copy(y_ref.at[last, now], yb.at[now], fetch)
    local.start()
    local.wait()
    for v in range(vch):
        gather_columns(now, lambda time, source: yb[now, source, v], 1, stat_count,
                       cols.at[pl.ds(0, 2 * depth)])
        real = jnp.dot(cols[pl.ds(0, depth), :], stacked[pl.ds(0, inputs), :],
                       preferred_element_type=jnp.float32)
        imag = jnp.dot(cols[pl.ds(depth, depth), :], stacked[pl.ds(inputs, inputs), :],
                       preferred_element_type=jnp.float32)
        place_beams(last, v, real + imag)
    @pl.loop(0, beams.shape[0] // 256)
    def _(n):
        at = pl.ds(pl.multiple_of(n * 256, 256), 256)
        lines[at, :] = beams[at, :].astype(jnp.bfloat16)

    out = pltpu.make_async_copy(lines, beam_ref, store.at[0])
    out.start()
    for number in range(peers):
        for copy in forward(y_ref.at[last, now, sources[number]], last, sources[number], number):
            copy.wait()
    for copy in forward(spec.at[last, me], last, me, peers):
        copy.wait()
    for number in range(close):
        issue(0, number).wait_send()
    for level in range(len(levels)):
        for copy in level_copies(level):
            copy.wait_send()
    for v in range(vch):
        keep_sums(v).wait()
    out.wait()


def front(voltages, weights, stat_count, time_count, local_vch):
    _, rows, items, points = voltages.shape
    inner = points // RADIX
    dma = pltpu.SemaphoreType.DMA
    width = 2 * rows
    inputs = stat_count * rows
    mine = inputs // time_count
    beams = weights.shape[1]
    peers = dma((stat_count,))
    each = dma((items, stat_count))
    over = dma((items, time_count, stat_count))
    block = (local_vch, AVG, width)
    lined = voltages.reshape(2, rows, items, points // 128, 128).transpose(0, 1, 3, 2, 4)
    lined = lined.reshape(2, rows, points // 128 * items, 128)
    matrix, turns = dft_tables(points)
    hbm = pl.BlockSpec(memory_space=pl.ANY)
    sums = (local_vch, 2 * mine, inputs)
    formed = (local_vch * AVG * items * 2 * beams // 128, 128)
    return pl.pallas_call(
        functools.partial(front_kernel, stat_count, time_count),
        in_specs=[pl.BlockSpec(memory_space=pltpu.HBM)] * 4,
        out_specs=[hbm, hbm, hbm],
        out_shape=[
            jax.ShapeDtypeStruct((items, time_count, stat_count) + block, jnp.bfloat16),
            jax.ShapeDtypeStruct(sums, jnp.bfloat16),
            jax.ShapeDtypeStruct(formed, jnp.bfloat16),
        ],
        scratch_shapes=[
            pltpu.VMEM(matrix.shape, matrix.dtype),
            pltpu.VMEM(turns.shape, turns.dtype),
            pltpu.VMEM(weights.shape, weights.dtype),
            pltpu.VMEM(lined.shape, jnp.bfloat16),
            pltpu.VMEM((2, rows * (lined.shape[2] + PAD), 128), jnp.float32),
            pltpu.VMEM((RADIX, width, 2 * inner), jnp.bfloat16),
            pltpu.VMEM((items, stat_count) + block, jnp.bfloat16),
            pltpu.VMEM((stat_count,) + weights.shape, weights.dtype),
            pltpu.VMEM((2 * inputs, 2 * beams), jnp.bfloat16),
            pltpu.VMEM((time_count, stat_count) + block, jnp.bfloat16),
            pltpu.VMEM((2 * time_count * AVG, inputs), jnp.bfloat16),
            pltpu.VMEM((2 * mine, 2 * time_count * AVG), jnp.bfloat16),
            pltpu.VMEM(sums, jnp.float32),
            pltpu.VMEM(sums, jnp.bfloat16),
            pltpu.VMEM(formed, jnp.float32),
            pltpu.VMEM(formed, jnp.bfloat16),
            dma((3,)), dma((GROUPS,)), dma, each, each, peers, peers, over, over, dma((items,)), dma, dma((1 + local_vch,)),
        ],
        compiler_params=pltpu.CompilerParams(
            collective_id=0, has_side_effects=True, vmem_limit_bytes=63 * 1024 * 1024),
        name="front",
    )(lined, matrix, turns, weights)


def finish_kernel(scale, y_ref, acc_ref, lines_ref, vis_ref, beam_ref,
                  y, acc, lines, vis, cols, left, take, some, give, pass_on):
    now = lax.axis_index("tm")
    times, sources, vch, depth, width = y.shape
    mine, groups = vis.shape[1], vis.shape[2]
    inputs = cols.shape[1]
    last = y_ref.shape[0] - 1
    run = mine // PIECES

    def ready(v):
        return [pltpu.make_async_copy(y_ref.at[last, :, :, v], y.at[:, :, v], take.at[v]),
                pltpu.make_async_copy(acc_ref.at[v], acc.at[v], some.at[v])]

    for v in range(vch):
        for copy in ready(v):
            copy.start()
    bring = pltpu.make_async_copy(lines_ref, lines, pass_on.at[0])
    bring.start()

    def result(v, step):
        rows = pl.ds(step * run, run)
        return pltpu.make_async_copy(vis.at[v, rows], vis_ref.at[rows, v], give.at[v, step])

    for v in range(vch):
        for copy in ready(v)[:1]:
            copy.wait()
        gather_columns(now, lambda time, source: y[time, source, v], times, sources, cols)
        turn_rows(now, cols, left, run)
        for copy in ready(v)[1:]:
            copy.wait()
        flat = vis.at[v].reshape(mine * groups, 128)

        @pl.loop(0, PIECES)
        def _(step):
            rows = pl.ds(pl.multiple_of(step * 2 * run, 2 * run), 2 * run)
            for n in range(inputs // BLOCK):
                at = pl.ds(n * BLOCK, BLOCK)
                value = jnp.dot(left[rows, :], cols[:, at], preferred_element_type=jnp.float32)
                for q in range(2):
                    mates = pl.ds(pl.multiple_of(q * mine + step * run, run), run)
                    whole = scale * (acc[v, mates, at].astype(jnp.float32) + value[q * run:(q + 1) * run])
                    for part in range(BLOCK // 128):
                        row = step * run * groups + (n * (BLOCK // 128) + part) * 2 + q
                        flat[pl.ds(row, run, stride=groups), :] = whole[:, part * 128:part * 128 + 128]
            result(v, step).start()

        if v == 0:
            bring.wait()
            hand = pltpu.make_async_copy(lines, beam_ref, pass_on.at[1])
            hand.start()
    for v in range(vch):
        for step in range(PIECES):
            result(v, step).wait()
    hand.wait()


def finish(spread, sums, lines, scale):
    _, times, sources, vch, fine, width = spread.shape
    mine = sums.shape[1] // 2
    inputs = sums.shape[2]
    groups = 2 * inputs // 128
    dma = pltpu.SemaphoreType.DMA
    hbm = pl.BlockSpec(memory_space=pl.ANY)
    return pl.pallas_call(
        functools.partial(finish_kernel, scale),
        in_specs=[hbm] * 3,
        out_specs=[hbm] * 2,
        scratch_shapes=[
            pltpu.VMEM(spread.shape[1:], spread.dtype),
            pltpu.VMEM(sums.shape, sums.dtype),
            pltpu.VMEM(lines.shape, lines.dtype),
            pltpu.VMEM((vch, mine, groups, 128), jnp.float32),
            pltpu.VMEM((2 * times * fine, inputs), jnp.bfloat16),
            pltpu.VMEM((2 * mine, 2 * times * fine), jnp.bfloat16),
            dma((vch,)), dma((vch,)), dma((vch, PIECES)), dma((2,)),
        ],
        out_shape=[
            jax.ShapeDtypeStruct((mine, vch, groups, 128), jnp.float32),
            jax.ShapeDtypeStruct(lines.shape, lines.dtype),
        ],
        compiler_params=pltpu.CompilerParams(vmem_limit_bytes=63 * 1024 * 1024),
        name="finish",
    )(spread, sums, lines)


def fast_body(voltages, beam_weights):
    stat_count = lax.axis_size("stat")
    time_count = lax.axis_size("tm")
    _, rows, items, points = voltages.shape
    beams_count = beam_weights.shape[2]
    local_vch = points // stat_count // AVG
    width = 2 * rows
    spread, sums, beams = front(
        voltages, beam_weights.reshape(width, beams_count), stat_count, time_count, local_vch)
    scale = 1.0 / (items * time_count * AVG)
    vis, beams = finish(spread, sums, beams, scale)
    beams = beams.reshape(local_vch * AVG, items, beams_count // 128, 2, 128).transpose(0, 1, 3, 2, 4)
    beams = beams.reshape(local_vch * AVG, items, 2, beams_count)
    vis = vis.reshape(vis.shape[0], local_vch, -1, 2, 128).transpose(0, 1, 3, 2, 4)
    return beams, vis.reshape(vis.shape[0], local_vch, 2, stat_count * rows)


def fits_tiles(mesh, voltages):
    _, inputs, spectra, points = voltages.shape
    rows = inputs // mesh.shape["stat"]
    mine = inputs // mesh.shape["tm"]
    share = points // mesh.shape["stat"]
    even = mesh.shape["stat"] & (mesh.shape["stat"] - 1) == 0 and mesh.shape["stat"] == 16
    return even and 2 * rows == 128 and mine % 128 == 0 and share % AVG == 0 and 2 <= spectra // mesh.shape["tm"] <= 4 and mesh.shape["tm"] == 2


def solution(mesh):
    def whole(voltages, beam_weights):
        return jax.shard_map(
            fast_body if fits_tiles(mesh, voltages) else body,
            mesh=mesh,
            in_specs=(P(None, "stat", "tm", None), P(None, "stat", None)),
            out_specs=(P("stat", "tm", None, None), P("tm", "stat", None, None)),
            check_vma=False,
        )(voltages, beam_weights)

    return whole
```

```python
import functools
import math

import jax
import jax.numpy as jnp
import numpy as np
from jax import lax
from jax.experimental import pallas as pl
from jax.experimental.pallas import tpu as pltpu
from jax.sharding import PartitionSpec as P

NA = 16
NB = 256
AVG = 128


def dft_block(length):
    index = jnp.arange(length, dtype=jnp.int32)
    product = index[:, None] * index[None, :] % length
    angle = product.astype(jnp.float32) * (2.0 * math.pi / length)
    cosine = jnp.cos(angle)
    sine = jnp.sin(angle)
    return jnp.stack([jnp.stack([cosine, -sine]), jnp.stack([sine, cosine])])


def fine_spectra(voltages):
    block_inputs = voltages.shape[1]
    spectra_count = voltages.shape[2]
    signal = voltages.astype(jnp.float32).reshape(2, block_inputs, spectra_count, NA, NB)
    first = jnp.einsum("poak,pisab->osikb", dft_block(NA), signal, precision=lax.Precision.HIGH)
    outer_index = jnp.arange(NA, dtype=jnp.int32)
    inner_index = jnp.arange(NB, dtype=jnp.int32)
    rotation = (outer_index[:, None] * inner_index[None, :] % (NA * NB)).astype(jnp.float32) * (
        2.0 * math.pi / (NA * NB)
    )
    cos_twist = jnp.cos(rotation)
    sin_twist = jnp.sin(rotation)
    rotated = jnp.stack(
        [first[0] * cos_twist + first[1] * sin_twist, first[1] * cos_twist - first[0] * sin_twist]
    )
    final = jnp.einsum("osikb,ocbq->csiqk", rotated, dft_block(NB), precision=lax.Precision.HIGH)
    norm_factor = 1.0 / math.sqrt(NA * NB)
    return (
        (final * norm_factor).reshape(2, spectra_count, block_inputs, NA * NB).astype(jnp.bfloat16)
    )


def stack_weights(weights):
    return jnp.stack(
        [jnp.stack([weights[0], weights[1]], 1), jnp.stack([-weights[1], weights[0]], 1)], 0
    )


def body(voltages, beam_weights):
    stat_count = lax.axis_size("stat")
    time_count = lax.axis_size("tm")
    block_inputs = voltages.shape[1]
    spectra = fine_spectra(voltages)
    spectra_count = spectra.shape[1]
    channel_share = NA * NB // stat_count
    all_weights = lax.all_gather(beam_weights, "stat", axis=1, tiled=True)
    full_stack = stack_weights(all_weights)
    turned = lax.all_to_all(spectra, "stat", split_axis=3, concat_axis=2, tiled=True)
    item_count = turned.shape[1]

    def add_block(block_index, running):
        offset = (block_index * block_inputs).astype(jnp.int32)
        spec_block = lax.dynamic_slice_in_dim(turned, offset, block_inputs, 2)
        weight_block = lax.dynamic_slice_in_dim(full_stack, offset, block_inputs, 1)
        partial_value = jnp.einsum(
            "psic,piqb->csqb", spec_block, weight_block, preferred_element_type=jnp.float32
        )
        rounded = lax.optimization_barrier(partial_value.astype(jnp.bfloat16))
        return running + rounded.astype(jnp.float32)

    initial = jnp.zeros((turned.shape[3], item_count, 2, beam_weights.shape[2]), jnp.float32)
    beams = lax.fori_loop(0, stat_count, add_block, initial).astype(jnp.bfloat16)
    local_vch = channel_share // AVG
    scale = 1.0 / (spectra_count * time_count * AVG)
    split = turned.reshape(2, spectra_count, stat_count * block_inputs, local_vch, AVG)
    real_gram = jnp.einsum("psiva,psjva->ivj", split, split, preferred_element_type=jnp.float32)
    mixed = jnp.einsum("siva,sjva->ivj", split[1], split[0], preferred_element_type=jnp.float32)
    mixed = mixed - jnp.einsum(
        "siva,sjva->ivj", split[0], split[1], preferred_element_type=jnp.float32
    )
    visibilities = lax.psum_scatter(
        (jnp.stack([real_gram, mixed], axis=2) * scale).astype(jnp.bfloat16),
        "tm",
        scatter_dimension=0,
        tiled=True,
    ).astype(jnp.float32)
    return (beams, visibilities)

RADIX = 8


def dft_tables(points):
    inner = points // RADIX
    index = np.arange(inner)
    angle = 2.0 * np.pi * (index[:, None] * index[None, :] % inner) / inner
    scale = 1.0 / math.sqrt(points)
    matrix = np.concatenate([np.cos(angle), np.sin(angle)], 1) * scale
    turn = 2.0 * np.pi * (np.arange(RADIX)[:, None] * index[None, :]) / points
    return (
        jnp.asarray(matrix, jnp.bfloat16),
        jnp.asarray(np.stack([np.cos(turn), np.sin(turn)]), jnp.float32),
    )


def cadd(a, b):
    return a[0] + b[0], a[1] + b[1]


def csub(a, b):
    return a[0] - b[0], a[1] - b[1]


def times_minus_i(a):
    return a[1], -a[0]


def radix4(a):
    s02, d02 = cadd(a[0], a[2]), csub(a[0], a[2])
    s13, d13 = cadd(a[1], a[3]), times_minus_i(csub(a[1], a[3]))
    return [cadd(s02, s13), cadd(d02, d13), csub(s02, s13), csub(d02, d13)]


def radix8(a):
    even, odd = radix4(a[0::2]), radix4(a[1::2])
    root = math.sqrt(0.5)
    o1, o2, o3 = odd[1], times_minus_i(odd[2]), odd[3]
    o1 = ((o1[0] + o1[1]) * root, (o1[1] - o1[0]) * root)
    o3 = ((o3[1] - o3[0]) * root, (-o3[0] - o3[1]) * root)
    odd = [odd[0], o1, o2, o3]
    return [cadd(e, o) for e, o in zip(even, odd)] + [csub(e, o) for e, o in zip(even, odd)]


def first_stage(x_ref, item, items, cos_ref, sin_ref, mid):
    rows = mid.shape[1] // 2
    inner = mid.shape[2] // 2
    held = x_ref.shape[1] // rows
    chunk = 16

    @pl.loop(0, rows // chunk)
    def _(step):
        at = pl.ds(pl.multiple_of(step * chunk, chunk), chunk)
        low = pl.ds(pl.multiple_of(rows + step * chunk, chunk), chunk)
        for lane in range(0, inner, 128):
            parts = []
            for n1 in range(RADIX):
                row = (n1 * inner + lane) // 128 * items + item
                cut = pl.ds(step * chunk * held + row, chunk, stride=held)
                parts.append((x_ref[0, cut, :], x_ref[1, cut, :]))
            for k1, (re, im) in enumerate(radix8(parts)):
                if k1:
                    c, s = cos_ref[k1:k1 + 1, lane:lane + 128], sin_ref[k1:k1 + 1, lane:lane + 128]
                    re, im = re * c + im * s, im * c - re * s
                re, im = re.astype(jnp.bfloat16), im.astype(jnp.bfloat16)
                left, right = pl.ds(lane, 128), pl.ds(inner + lane, 128)
                mid[k1, at, left] = re
                mid[k1, at, right] = im
                mid[k1, low, left] = im
                mid[k1, low, right] = -re


def second_stage(mid, m_ref, out_ref, part=0, parts=1):
    targets, vch, depth, width = out_ref.shape
    targets //= parts
    some = m_ref.shape[0] // parts
    first = pl.ds(part * targets, targets)
    wanted = pl.ds(part * some, some) if parts == 1 else pl.ds(pl.multiple_of(part * some, 128), some)
    fine = depth // RADIX

    @pl.loop(0, RADIX // 2)
    def _(half):
        pair = mid[pl.ds(2 * half, 2)].reshape(2 * width, mid.shape[2])
        done = lax.dot_general(
            m_ref[wanted, :], pair, (((1,), (1,)), ((), ())), preferred_element_type=jnp.float32
        ).astype(jnp.bfloat16)
        for k1 in range(2):
            at = pl.ds(pl.multiple_of((2 * half + k1) * fine, fine), fine)
            out_ref[first, :, at, :] = done[:, k1 * width:(k1 + 1) * width].reshape(targets, vch, fine, width)


def near_and_far(count):
    half = count // 2
    far = [(half, (j // 2 + j % 2 * (half // 2)) % half) for j in range(half)]
    near = []
    half //= 2
    while half:
        near = [(half, j) for j in range(half)] + near
        half //= 2
    return near, far


FAR_WINDOW = 6
NEAR_WINDOW = 3
LATE = 3
AHEAD = 2
BLOCK = 256
GROUPS = 4
PAD = 8
PIECES = 4


def gather_columns(now, take, times, sources, cols):
    depth, half = AVG, cols.shape[1] // sources
    total = times * depth
    for time in range(times):
        for source in range(0, sources, 2):
            a, b = take(time, source), take(time, source + 1)
            out = pl.ds(source * half, 2 * half)
            cols[pl.ds(time * depth, depth), out] = jnp.concatenate([a[:, :half], b[:, :half]], 1)
            cols[pl.ds(total + time * depth, depth), out] = jnp.concatenate([a[:, half:], b[:, half:]], 1)


def turn_rows(now, cols, left, run=None):
    total = cols.shape[0] // 2
    mine = left.shape[0] // 2
    run = run or mine
    for tile in range(0, mine, 128):
        place = tile // run * 2 * run + tile % run
        at = pl.ds(pl.multiple_of(now * mine + tile, 128), 128)
        re = (cols[pl.ds(0, total), at]).T
        im = (cols[pl.ds(total, total), at]).T
        left[pl.ds(place, 128), pl.ds(0, total)] = re
        left[pl.ds(place, 128), pl.ds(total, total)] = im
        left[pl.ds(place + run, 128), pl.ds(0, total)] = im
        left[pl.ds(place + run, 128), pl.ds(total, total)] = -re


def front_kernel(stat_count, time_count, x_ref, m_hbm, turn_hbm, w_hbm, y_ref, acc_ref, beam_ref,
                 m_ref, turn_ref, w_ref, xv, wide_x, mid, spec, wg, stacked, yb, cols, left, acc, packed, beams, lines,
                 const, loc, wloc, send, recv, wsend, wrecv, fsend, frecv, keep, fetch, store):
    me, now = lax.axis_index("stat"), lax.axis_index("tm")
    items, _, vch, depth, width = spec.shape
    last = items - 1
    half = width // 2
    mine = left.shape[0] // 2
    inputs = cols.shape[1]
    total = cols.shape[0] // 2
    wide = w_ref.shape[1]
    cos_ref, sin_ref = turn_ref.at[0], turn_ref.at[1]
    wput = pltpu.make_async_copy(w_ref, wg.at[me], wloc)

    barrier = pltpu.get_barrier_semaphore()
    for k in range(1, stat_count):
        pl.semaphore_signal(barrier, inc=1, device_id={"stat": lax.rem(me + k, stat_count)},
                            device_id_type=pl.DeviceIdType.MESH)
    for j in range(1, time_count):
        pl.semaphore_signal(barrier, inc=1, device_id={"tm": lax.rem(now + j, time_count)},
                            device_id_type=pl.DeviceIdType.MESH)

    held = x_ref.shape[2]
    group = x_ref.shape[1] // GROUPS
    tables = [pltpu.make_async_copy(src, dst, const.at[n])
              for n, (src, dst) in enumerate([(turn_hbm, turn_ref), (w_hbm, w_ref), (m_hbm, m_ref)])]
    tables[1].start()
    loads = []
    for c in range(GROUPS):
        at = pl.ds(c * group, group)
        loads.append(pltpu.make_async_copy(x_ref.at[:, at], xv.at[:, at], loc.at[c]))
        loads[-1].start()
    tables[0].start()
    tables[2].start()

    near, far = near_and_far(stat_count)
    order = near + far
    peers, close = len(order), len(near)

    def partner(k, sign):
        half = k[0]
        other = me // half + 1 - 2 * lax.rem(me // half, 2)
        return other * half + lax.rem(lax.rem(me, half) + half + sign * k[1], half)

    sends = [partner(k, 1) for k in order]
    sources = [partner(k, -1) for k in order]

    def to(src, dst, there, out_sem, in_sem):
        return pltpu.make_async_remote_copy(
            src_ref=src, dst_ref=dst, send_sem=out_sem, recv_sem=in_sem,
            device_id={"stat": there}, device_id_type=pl.DeviceIdType.MESH)

    def forward(src, s, source, slot):
        return [pltpu.make_async_remote_copy(
            src_ref=src, dst_ref=y_ref.at[s, now, source],
            send_sem=fsend.at[s, j, slot], recv_sem=frecv.at[s, j, slot],
            device_id={"tm": lax.rem(now + j, time_count)}, device_id_type=pl.DeviceIdType.MESH)
            for j in range(1, time_count)]

    def issue(s, number):
        there = sends[number]
        return to(spec.at[s, there], y_ref.at[s, now, me], there, send.at[s, number], recv.at[s, number])

    def put(s):
        return pltpu.make_async_copy(spec.at[s, me], y_ref.at[s, now, me], keep.at[s])

    def take(s, number):
        source = sources[number]
        to(spec.at[s, source], y_ref.at[s, now, source], source, send.at[s, number], recv.at[s, number]).wait_recv()
        for copy in forward(y_ref.at[s, now, source], s, source, number):
            copy.start()

    def finish(s):
        put(s).wait()
        for number in range(peers):
            for copy in forward(y_ref.at[s, now, sources[number]], s, sources[number], number):
                copy.wait()
        for copy in forward(spec.at[s, me], s, me, peers):
            copy.wait()

    def own_block(s):
        for copy in forward(spec.at[s, me], s, me, peers):
            copy.start()
        put(s).start()

    def transform(s, between=None):
        first_stage(wide_x, s, items, cos_ref, sin_ref, mid)
        if between:
            between()
        second_stage(mid, m_ref, spec.at[s])
        own_block(s)

    levels = []
    reach = stat_count // 2
    while reach:
        levels.append(reach)
        reach //= 2

    def level_copies(level):
        reach = levels[level]
        period = 2 * reach
        other = partner((reach, 0), 1)
        made = []
        for turn in range(stat_count // period):
            block = lax.rem(me, period) + period * turn
            index = stat_count // period + turn
            made.append(to(wg.at[block] if level else w_ref, wg.at[block], other,
                           wsend.at[index], wrecv.at[index]))
        return made

    def start_level(level):
        if level:
            for copy in level_copies(level - 1):
                copy.wait_recv()
        else:
            wput.wait()
        for copy in level_copies(level):
            copy.start()

    def stack_weights_now():
        for copy in level_copies(len(levels) - 1):
            copy.wait_recv()
        for source in range(stat_count):
            upper = pl.ds(source * half, half)
            lower = pl.ds(inputs + source * half, half)
            stacked[upper, pl.ds(0, wide)] = wg[source, :half]
            stacked[upper, pl.ds(wide, wide)] = wg[source, half:]
            stacked[lower, pl.ds(0, wide)] = -wg[source, half:]
            stacked[lower, pl.ds(wide, wide)] = wg[source, :half]

    lanes = 2 * wide // 128
    fine = depth // RADIX

    def place_beams(s, v, value):
        for k1 in range(RADIX):
            rows = value[k1 * fine:(k1 + 1) * fine]
            for lane in range(lanes):
                q, tile = divmod(lane, lanes // 2)
                start = ((v * depth + k1) * items + s) * lanes + tile * 2 + q
                beams[pl.ds(start, fine, stride=RADIX * items * lanes), :] = rows[:, lane * 128:lane * 128 + 128]

    def form_beams(s, v, start):
        real = jnp.dot(cols[pl.ds(start, depth), :], stacked[pl.ds(0, inputs), :],
                       preferred_element_type=jnp.float32)
        imag = jnp.dot(cols[pl.ds(total + start, depth), :], stacked[pl.ds(inputs, inputs), :],
                       preferred_element_type=jnp.float32)
        place_beams(s, v, real + imag)

    def load(s):
        return pltpu.make_async_copy(y_ref.at[s], yb, fetch)

    def add_products(v, n):
        at = pl.ds(n * BLOCK, BLOCK)
        for q in range(2):
            rows = pl.ds(q * mine, mine)
            value = acc[v, rows, at] + jnp.dot(left[rows, :], cols[:, at], preferred_element_type=jnp.float32)
            acc[v, rows, at] = value
            packed[v, rows, at] = value.astype(packed.dtype)

    def keep_sums(v):
        return pltpu.make_async_copy(packed.at[v], acc_ref.at[v], store.at[1 + v])

    def correlate_part(s, part):
        parts = inputs // BLOCK
        if part == 0:
            finish(s)
            load(s).start()
            return
        if part == 1:
            load(s).wait()
        v, n = divmod(part - 1, parts)
        if v >= vch:
            return
        if n == 0:
            gather_columns(now, lambda time, source: yb[time, source, v], time_count, stat_count, cols)
            turn_rows(now, cols, left)
            form_beams(s, v, pl.multiple_of(now * depth, depth))
        add_products(v, n)
        if n == parts - 1:
            @pl.when(s == last - 1)
            def _():
                keep_sums(v).start()

    for c, load_x in enumerate(loads):
        load_x.wait()

        @pl.loop(c * group, (c + 1) * group)
        def _(row):
            at = pl.ds(pl.multiple_of(row * (held + PAD), 8), held)
            for p in range(2):
                wide_x[p, at, :] = xv[p, row].astype(jnp.float32)

    tables[1].wait()
    wput.start()
    pl.semaphore_wait(barrier, stat_count + time_count - 2)
    start_level(0)
    tables[0].wait()
    first_stage(wide_x, 0, items, cos_ref, sin_ref, mid)
    tables[2].wait()
    away = lax.rem(me // len(far) + 1, 2)
    second_stage(mid, m_ref, spec.at[0], away, 2)
    for number in range(FAR_WINDOW):
        issue(0, close + number).start()
    second_stage(mid, m_ref, spec.at[0], 1 - away, 2)
    own_block(0)
    for number in range(close):
        issue(0, number).start()

    def first_takes():
        for number in range(2):
            take(0, number)
        start_level(1)

    transform(1, first_takes)
    for number in range(NEAR_WINDOW):
        issue(1, number).start()
    for number in range(2, close):
        take(0, number)

    every = 1 + vch * (inputs // BLOCK)
    steps = len(far)
    spots = steps - LATE
    plan = [LATE + min(part * spots // every, spots - 1) for part in range(every)]

    @pl.loop(0, items)
    def _(s):
        for j in range(steps):
            take(s, close + j)
            issue(s, close + j).wait_send()
            if j + FAR_WINDOW < steps:
                issue(s, close + j + FAR_WINDOW).start()
            else:
                @pl.when(s < last)
                def _():
                    issue(s + 1, close + j + FAR_WINDOW - steps).start()
            if j < close:
                @pl.when(s < last)
                def _():
                    issue(s + 1, j).wait_send()
                    if j + NEAR_WINDOW < close:
                        issue(s + 1, j + NEAR_WINDOW).start()
                    else:
                        @pl.when(s + 1 < last)
                        def _():
                            issue(s + 2, j + NEAR_WINDOW - close).start()
                    take(s + 1, j)
            if j % 3 == 2 and j // 3 + 2 < len(levels):
                @pl.when(s == 0)
                def _():
                    start_level(j // 3 + 2)
            if j == AHEAD:
                @pl.when(s + 1 < last)
                def _():
                    transform(s + 2)
            if j == 4:
                @pl.when(s == 0)
                def _():
                    acc[...] = jnp.zeros(acc.shape, acc.dtype)
            if j == 1:
                @pl.when(s == 1)
                def _():
                    stack_weights_now()
            parts = [part for part, spot in enumerate(plan) if spot == j]
            if parts:
                @pl.when(s > 0)
                def _():
                    for part in parts:
                        correlate_part(s - 1, part)

    put(last).wait()
    local = pltpu.make_async_copy(y_ref.at[last, now], yb.at[now], fetch)
    local.start()
    local.wait()
    for v in range(vch):
        gather_columns(now, lambda time, source: yb[now, source, v], 1, stat_count,
                       cols.at[pl.ds(0, 2 * depth)])
        real = jnp.dot(cols[pl.ds(0, depth), :], stacked[pl.ds(0, inputs), :],
                       preferred_element_type=jnp.float32)
        imag = jnp.dot(cols[pl.ds(depth, depth), :], stacked[pl.ds(inputs, inputs), :],
                       preferred_element_type=jnp.float32)
        place_beams(last, v, real + imag)
    @pl.loop(0, beams.shape[0] // 256)
    def _(n):
        at = pl.ds(pl.multiple_of(n * 256, 256), 256)
        lines[at, :] = beams[at, :].astype(jnp.bfloat16)

    out = pltpu.make_async_copy(lines, beam_ref, store.at[0])
    out.start()
    for number in range(peers):
        for copy in forward(y_ref.at[last, now, sources[number]], last, sources[number], number):
            copy.wait()
    for copy in forward(spec.at[last, me], last, me, peers):
        copy.wait()
    for number in range(close):
        issue(0, number).wait_send()
    for level in range(len(levels)):
        for copy in level_copies(level):
            copy.wait_send()
    for v in range(vch):
        keep_sums(v).wait()
    out.wait()


def front(voltages, weights, stat_count, time_count, local_vch):
    _, rows, items, points = voltages.shape
    inner = points // RADIX
    dma = pltpu.SemaphoreType.DMA
    width = 2 * rows
    inputs = stat_count * rows
    mine = inputs // time_count
    beams = weights.shape[1]
    peers = dma((stat_count,))
    each = dma((items, stat_count))
    over = dma((items, time_count, stat_count))
    block = (local_vch, AVG, width)
    lined = voltages.reshape(2, rows, items, points // 128, 128).transpose(0, 1, 3, 2, 4)
    lined = lined.reshape(2, rows, points // 128 * items, 128)
    matrix, turns = dft_tables(points)
    hbm = pl.BlockSpec(memory_space=pl.ANY)
    sums = (local_vch, 2 * mine, inputs)
    formed = (local_vch * AVG * items * 2 * beams // 128, 128)
    return pl.pallas_call(
        functools.partial(front_kernel, stat_count, time_count),
        in_specs=[pl.BlockSpec(memory_space=pltpu.HBM)] * 4,
        out_specs=[hbm, hbm, hbm],
        out_shape=[
            jax.ShapeDtypeStruct((items, time_count, stat_count) + block, jnp.bfloat16),
            jax.ShapeDtypeStruct(sums, jnp.bfloat16),
            jax.ShapeDtypeStruct(formed, jnp.bfloat16),
        ],
        scratch_shapes=[
            pltpu.VMEM(matrix.shape, matrix.dtype),
            pltpu.VMEM(turns.shape, turns.dtype),
            pltpu.VMEM(weights.shape, weights.dtype),
            pltpu.VMEM(lined.shape, jnp.bfloat16),
            pltpu.VMEM((2, rows * (lined.shape[2] + PAD), 128), jnp.float32),
            pltpu.VMEM((RADIX, width, 2 * inner), jnp.bfloat16),
            pltpu.VMEM((items, stat_count) + block, jnp.bfloat16),
            pltpu.VMEM((stat_count,) + weights.shape, weights.dtype),
            pltpu.VMEM((2 * inputs, 2 * beams), jnp.bfloat16),
            pltpu.VMEM((time_count, stat_count) + block, jnp.bfloat16),
            pltpu.VMEM((2 * time_count * AVG, inputs), jnp.bfloat16),
            pltpu.VMEM((2 * mine, 2 * time_count * AVG), jnp.bfloat16),
            pltpu.VMEM(sums, jnp.float32),
            pltpu.VMEM(sums, jnp.bfloat16),
            pltpu.VMEM(formed, jnp.float32),
            pltpu.VMEM(formed, jnp.bfloat16),
            dma((3,)), dma((GROUPS,)), dma, each, each, peers, peers, over, over, dma((items,)), dma, dma((1 + local_vch,)),
        ],
        compiler_params=pltpu.CompilerParams(
            collective_id=0, has_side_effects=True, vmem_limit_bytes=63 * 1024 * 1024),
        name="front",
    )(lined, matrix, turns, weights)


def finish_kernel(scale, y_ref, acc_ref, lines_ref, vis_ref, beam_ref,
                  y, acc, lines, vis, cols, left, take, some, give, pass_on):
    now = lax.axis_index("tm")
    times, sources, vch, depth, width = y.shape
    mine, groups = vis.shape[1], vis.shape[2]
    inputs = cols.shape[1]
    last = y_ref.shape[0] - 1
    run = mine // PIECES

    def ready(v):
        return [pltpu.make_async_copy(y_ref.at[last, :, :, v], y.at[:, :, v], take.at[v]),
                pltpu.make_async_copy(acc_ref.at[v], acc.at[v], some.at[v])]

    for v in range(vch):
        for copy in ready(v):
            copy.start()
    bring = pltpu.make_async_copy(lines_ref, lines, pass_on.at[0])
    bring.start()

    def result(v, step):
        rows = pl.ds(step * run, run)
        return pltpu.make_async_copy(vis.at[v, rows], vis_ref.at[rows, v], give.at[v, step])

    for v in range(vch):
        for copy in ready(v)[:1]:
            copy.wait()
        gather_columns(now, lambda time, source: y[time, source, v], times, sources, cols)
        turn_rows(now, cols, left, run)
        for copy in ready(v)[1:]:
            copy.wait()
        flat = vis.at[v].reshape(mine * groups, 128)

        @pl.loop(0, PIECES)
        def _(step):
            rows = pl.ds(pl.multiple_of(step * 2 * run, 2 * run), 2 * run)
            for n in range(inputs // BLOCK):
                at = pl.ds(n * BLOCK, BLOCK)
                value = jnp.dot(left[rows, :], cols[:, at], preferred_element_type=jnp.float32)
                for q in range(2):
                    mates = pl.ds(pl.multiple_of(q * mine + step * run, run), run)
                    whole = scale * (acc[v, mates, at].astype(jnp.float32) + value[q * run:(q + 1) * run])
                    for part in range(BLOCK // 128):
                        row = step * run * groups + (n * (BLOCK // 128) + part) * 2 + q
                        flat[pl.ds(row, run, stride=groups), :] = whole[:, part * 128:part * 128 + 128]
            result(v, step).start()

        if v == 0:
            bring.wait()
            hand = pltpu.make_async_copy(lines, beam_ref, pass_on.at[1])
            hand.start()
    for v in range(vch):
        for step in range(PIECES):
            result(v, step).wait()
    hand.wait()


def finish(spread, sums, lines, scale):
    _, times, sources, vch, fine, width = spread.shape
    mine = sums.shape[1] // 2
    inputs = sums.shape[2]
    groups = 2 * inputs // 128
    dma = pltpu.SemaphoreType.DMA
    hbm = pl.BlockSpec(memory_space=pl.ANY)
    return pl.pallas_call(
        functools.partial(finish_kernel, scale),
        in_specs=[hbm] * 3,
        out_specs=[hbm] * 2,
        scratch_shapes=[
            pltpu.VMEM(spread.shape[1:], spread.dtype),
            pltpu.VMEM(sums.shape, sums.dtype),
            pltpu.VMEM(lines.shape, lines.dtype),
            pltpu.VMEM((vch, mine, groups, 128), jnp.float32),
            pltpu.VMEM((2 * times * fine, inputs), jnp.bfloat16),
            pltpu.VMEM((2 * mine, 2 * times * fine), jnp.bfloat16),
            dma((vch,)), dma((vch,)), dma((vch, PIECES)), dma((2,)),
        ],
        out_shape=[
            jax.ShapeDtypeStruct((mine, vch, groups, 128), jnp.float32),
            jax.ShapeDtypeStruct(lines.shape, lines.dtype),
        ],
        compiler_params=pltpu.CompilerParams(vmem_limit_bytes=63 * 1024 * 1024),
        name="finish",
    )(spread, sums, lines)


def fast_body(voltages, beam_weights):
    stat_count = lax.axis_size("stat")
    time_count = lax.axis_size("tm")
    _, rows, items, points = voltages.shape
    beams_count = beam_weights.shape[2]
    local_vch = points // stat_count // AVG
    width = 2 * rows
    spread, sums, beams = front(
        voltages, beam_weights.reshape(width, beams_count), stat_count, time_count, local_vch)
    scale = 1.0 / (items * time_count * AVG)
    vis, beams = finish(spread, sums, beams, scale)
    beams = beams.reshape(local_vch * AVG, items, beams_count // 128, 2, 128).transpose(0, 1, 3, 2, 4)
    beams = beams.reshape(local_vch * AVG, items, 2, beams_count)
    vis = vis.reshape(vis.shape[0], local_vch, -1, 2, 128).transpose(0, 1, 3, 2, 4)
    return beams, vis.reshape(vis.shape[0], local_vch, 2, stat_count * rows)


def fits_tiles(mesh, voltages):
    _, inputs, spectra, points = voltages.shape
    rows = inputs // mesh.shape["stat"]
    mine = inputs // mesh.shape["tm"]
    share = points // mesh.shape["stat"]
    even = mesh.shape["stat"] & (mesh.shape["stat"] - 1) == 0 and mesh.shape["stat"] == 16
    return even and 2 * rows == 128 and mine % 128 == 0 and share % AVG == 0 and 2 <= spectra // mesh.shape["tm"] <= 4 and mesh.shape["tm"] == 2


def solution(mesh):
    def whole(voltages, beam_weights):
        return jax.shard_map(
            fast_body if fits_tiles(mesh, voltages) else body,
            mesh=mesh,
            in_specs=(P(None, "stat", "tm", None), P(None, "stat", None)),
            out_specs=(P("stat", "tm", None, None), P("tm", "stat", None, None)),
            check_vma=False,
        )(voltages, beam_weights)

    return whole
```
